32 devices in a mesh: dp: 2 (over x), expert: 16 (over z, y, core).
Axes of the slice: x: 2, y: 2, z: 4, core: 2. Of those that a mesh axis runs over, the one named last changes fastest.
Arguments:
- tokens: bfloat16 [4096, 1024], P(('dp', 'expert')), may hold values from -6 to 6
- routes: int32 [4096, 4], P(('dp', 'expert')), may hold values from 0 to 15, all different within a row; in each aligned block of 128 rows (0 to 127, 128 to 255, ...) at most 40 rows name the same one
- gates: float32 [4096, 4], P(('dp', 'expert')), may hold values from 0.05 to 0.5
- gate_weight: bfloat16 [16, 1024, 384], P('expert', 'dp'), may hold values from -0.1875 to 0.1875
- up_weight: bfloat16 [16, 1024, 384], P('expert', 'dp'), may hold values from -0.1875 to 0.1875
- down_weight: bfloat16 [16, 1024, 384], P('expert', 'dp'), may hold values from -0.3125 to 0.3125
- cotangent: bfloat16 [4096, 1024], P(('dp', 'expert')), may hold values from -1.1953125 to 1.1953125
Outputs:
- mixed: bfloat16 [4096, 1024], P(('dp', 'expert'))
- token_grads: bfloat16 [4096, 1024], P(('dp', 'expert'))
- gate_grads: float32 [4096, 4], P(('dp', 'expert'))
- gate_weight_grad: float32 [16, 1024, 384], P('expert', 'dp')
- up_weight_grad: float32 [16, 1024, 384], P('expert', 'dp')
- down_weight_grad: float32 [16, 1024, 384], P('expert', 'dp')
The draws below stay inside these ranges and needn't reach their ends.
Inputs may be any that keep to these rules, and one draw needn't show every extreme that they name: `routes`: each row names 4 different experts. In each aligned block of 128 rows (the tokens of one device) no expert is named by more than 40 rows, and in some blocks one expert is named by exactly 40 rows.
All inputs are finite; a program needn't handle non-finite values.
Results may differ from the reference program's by a relative error of at most 0.0065.
Values may be sent and summed in bfloat16 or wider, within the bound.
No kernel may reach another device: no remote copies, remote signals or barrier semaphores. Data moves between devices by JAX's collectives and lax.ppermute only.
A program may use at most 64 MiB of HBM per device.

```python
import math
import jax
import jax.numpy as jnp
import numpy as np
from jax import lax

D = 1024
FF = 384
TOPK = 4
TOK_DEV = 128
EXPERTS = 16
CAP = 40
TOKENS = 4096
N_DP = 2
N_EXPERT = 16


def level_of(rng, dims, cuts, low, top_value):
    loudness, own = 1.0, jax.random.fold_in(rng, 6)
    for axis_at, blocks in cuts:
        draws = jnp.exp(jax.random.uniform(jax.random.fold_in(own, axis_at), (blocks,), jnp.float32, low / len(cuts), top_value / len(cuts)))
        loudness = loudness * jnp.repeat(draws, dims[axis_at] // blocks).reshape([-1 if axis == axis_at else 1 for axis in range(len(dims))])
    return loudness


def routed_block(own_key, own, number, rows, count, top, reach, lean):
    order = jax.random.permutation(own_key, count)
    heavy_load, ordinary = portions_of(count, rows * top, reach, lean, True), portions_of(count, rows * top, reach, lean, False)
    places = jnp.arange(count)

    def named(tallies, rotation):
        used = int((tallies > 0).sum())
        fixed = max(1, used // 4)
        passed = fixed + (places - fixed + rotation * (used - fixed)) % max(1, count - fixed)
        return jnp.zeros((count,), jnp.int32).at[order[jnp.where(places < fixed, places, passed)]].set(jnp.asarray(tallies, jnp.int32))

    tallies = jnp.where(number % 4 == 0, named(heavy_load, number // 4), named(ordinary, number - number // 4 - 1))
    mixed = jax.random.permutation(jax.random.fold_in(own, 3), count)
    giver, sink = mixed[0:count // 2 * 2:2], mixed[1:count // 2 * 2:2]
    margin = jnp.minimum(tallies[giver] - 1, reach - tallies[sink]) // 2
    margin = jnp.where((giver == order[0]) | (sink == order[0]) | (tallies[sink] == 0), 0, jnp.maximum(margin, 0))
    passed = jax.random.randint(jax.random.fold_in(own, 4), (count // 2,), 0, 1 << 20) % (margin + 1)
    tallies = tallies.at[giver].add(-passed).at[sink].add(passed)
    members = jnp.searchsorted(jnp.cumsum(tallies), jnp.arange(rows * top), side="right").astype(jnp.int32)
    grid = members.reshape(top, rows).T
    grid = grid[jax.random.permutation(jax.random.fold_in(own, 1), rows)]
    rotation = jax.random.randint(jax.random.fold_in(own, 2), (rows, 1), 0, top)
    return jnp.take_along_axis(grid, (jnp.arange(top)[None, :] + rotation) % top, axis=1)


def portions_of(amount, total, reach, skew, full):
    weights = [(1 << 20) // math.isqrt(rank ** skew) + 1 for rank in range(1, amount + 1)]
    largest = reach if full else min(reach, max(-(-total // amount), total * weights[0] // sum(weights)))
    least = 1 if total - largest >= amount - 1 else 0
    counts, rest = [largest] + [least] * (amount - 1), total - largest - least * (amount - 1)
    while rest > 0:
        candidates = [i for i in range(1, amount) if counts[i] < largest] or [i for i in range(1, amount) if counts[i] < reach]
        mass, budget = sum([weights[i] for i in candidates]), rest
        for i in candidates:
            addition = min(reach - counts[i], max(1, budget * weights[i] // mass), rest)
            counts[i] = counts[i] + addition
            rest = rest - addition
    return np.array(counts)


def scatter_about(key, shape, scale, limit, pieces=(), held_as=jnp.bfloat16):
    gain = level_of(key, shape, pieces, -0.22, 0.18) if pieces else 1.0
    result = jax.random.normal(key, shape, jnp.float32) * scale * gain
    return jnp.minimum(jnp.maximum(result, -limit), limit).astype(held_as)


def setup_inputs(seed: int = 0) -> dict:
    key_list = jax.random.split(jax.random.key(seed), 8)
    tokens = scatter_about(key_list[0], (TOKENS, D), 1.0, 6.0, ((0, 32),))
    routes_keys = jax.random.split(jax.random.fold_in(key_list[1], 1), TOKENS // TOK_DEV)
    routes_turns = jax.random.permutation(jax.random.fold_in(key_list[1], 3), TOKENS // TOK_DEV)
    routes = jax.vmap(lambda own, number: routed_block(jax.random.fold_in(key_list[1], 2), own, number, TOK_DEV, EXPERTS, TOPK, CAP, 2))(routes_keys, routes_turns).reshape((TOKENS, TOPK))
    gates = jnp.clip(0.05 + 0.45 * jax.random.uniform(key_list[2], (TOKENS, TOPK), jnp.float32) ** level_of(key_list[2], (TOKENS, TOPK), ((0, 32),), -0.2, 0.2), 0.05, 0.5)
    gate_weight = scatter_about(key_list[3], (EXPERTS, D, FF), D ** -0.5, 0.1875, ((0, 16), (1, 2)))
    up_weight = scatter_about(key_list[4], (EXPERTS, D, FF), D ** -0.5, 0.1875, ((0, 16), (1, 2)))
    down_weight = scatter_about(key_list[5], (EXPERTS, D, FF), FF ** -0.5, 0.3125, ((0, 16), (1, 2)))
    cotangent = scatter_about(key_list[6], (TOKENS, D), 0.2, 1.1953125, ((0, 32),))
    return dict(tokens=tokens, routes=routes, gates=gates, gate_weight=gate_weight, up_weight=up_weight, down_weight=down_weight, cotangent=cotangent)


def reference(tokens, routes, gates, gate_weight, up_weight, down_weight, cotangent):
    pair_count = TOK_DEV * TOPK
    slot_count = N_EXPERT * CAP
    grouped = routes.reshape(N_DP, N_EXPERT, pair_count)
    onehot = (grouped[..., None] == jnp.arange(EXPERTS, dtype=jnp.int32)).astype(jnp.int32)
    position = jnp.sum((jnp.cumsum(onehot, axis=2) - 1) * onehot, axis=3).astype(jnp.int32)
    slot_of = (jnp.arange(N_EXPERT, dtype=jnp.int32)[None, :, None] * CAP + position).astype(jnp.int32)
    pair_ids = jnp.arange(N_DP * N_EXPERT * pair_count, dtype=jnp.int32).reshape(N_DP, N_EXPERT, pair_count)
    group_ids = jnp.broadcast_to(jnp.arange(N_DP, dtype=jnp.int32)[:, None, None], grouped.shape)
    table = jnp.full((N_DP, EXPERTS, slot_count), -1, jnp.int32).at[group_ids, grouped, slot_of].set(pair_ids)
    flat_gates = gates.reshape(-1)

    def rounded_sum(left, right):
        left_groups = left.reshape(N_DP, slot_count, -1).astype(jnp.float32)
        right_groups = right.reshape(N_DP, slot_count, -1).astype(jnp.float32)
        per_group = jnp.einsum("nsd,nsf->ndf", left_groups, right_groups)
        rounded = lax.optimization_barrier(per_group.astype(jnp.bfloat16))
        return jnp.sum(rounded.astype(jnp.float32), axis=0)

    def per_expert(carry, expert_id):
        mixed_acc, grad_acc, gate_acc = carry
        pair_index = table[:, expert_id, :].reshape(-1)
        valid = pair_index >= 0
        safe_index = jnp.maximum(pair_index, 0).astype(jnp.int32)
        token_index = (safe_index // TOPK).astype(jnp.int32)
        rows_in = jnp.where(valid[:, None], tokens[token_index], jnp.zeros((), tokens.dtype))
        w_gate = gate_weight[expert_id]
        w_up = up_weight[expert_id]
        w_down = down_weight[expert_id]
        pre_gate = jnp.dot(rows_in, w_gate, preferred_element_type=jnp.float32)
        pre_up = jnp.dot(rows_in, w_up, preferred_element_type=jnp.float32)
        hidden = (jax.nn.silu(pre_gate) * pre_up).astype(jnp.bfloat16)
        expert_out = jnp.dot(hidden, w_down.T, preferred_element_type=jnp.float32).astype(jnp.bfloat16)
        out_float = expert_out.astype(jnp.float32)
        gate_rows = jnp.where(valid, flat_gates[safe_index], jnp.zeros((), flat_gates.dtype))
        cot_rows = cotangent[token_index].astype(jnp.float32)
        mixed_acc = mixed_acc.at[token_index].add(gate_rows[:, None] * out_float)
        gate_terms = jnp.sum(cot_rows * out_float, axis=1)
        gate_acc = gate_acc.at[safe_index].add(jnp.where(valid, gate_terms, jnp.zeros((), gate_terms.dtype)))
        scaled = (gate_rows[:, None] * cot_rows).astype(jnp.bfloat16)
        grad_hidden = jnp.dot(scaled, w_down, preferred_element_type=jnp.float32)
        sigma = jax.nn.sigmoid(pre_gate)
        d_gate = (grad_hidden * pre_up * sigma * (1.0 + pre_gate * (1.0 - sigma))).astype(jnp.bfloat16)
        d_up = (grad_hidden * pre_gate * sigma).astype(jnp.bfloat16)
        grad_rows = (jnp.dot(d_gate, w_gate.T, preferred_element_type=jnp.float32)
                     + jnp.dot(d_up, w_up.T, preferred_element_type=jnp.float32)).astype(jnp.bfloat16)
        grad_acc = grad_acc.at[token_index].add(grad_rows.astype(jnp.float32))
        grads = (rounded_sum(rows_in, d_gate), rounded_sum(rows_in, d_up), rounded_sum(scaled, hidden))
        return (mixed_acc, grad_acc, gate_acc), grads

    start = (jnp.zeros((TOKENS, D), jnp.float32), jnp.zeros((TOKENS, D), jnp.float32),
             jnp.zeros((TOKENS * TOPK,), jnp.float32))
    carry, grads = lax.scan(per_expert, start, jnp.arange(EXPERTS, dtype=jnp.int32))
    mixed_acc, grad_acc, gate_acc = carry
    return (mixed_acc.astype(jnp.bfloat16), grad_acc.astype(jnp.bfloat16), gate_acc.reshape(TOKENS, TOPK),
            grads[0], grads[1], grads[2])
```

```python
import functools

import jax
import jax.numpy as jnp
from jax import lax
from jax.experimental import pallas as pl
from jax.experimental.pallas import tpu as pltpu
from jax.sharding import PartitionSpec as P

BF = jnp.bfloat16
F32 = jnp.float32


def dot(left, right):
    return jnp.dot(left, right, preferred_element_type=F32)


def dot_rows(left, right):
    return lax.dot_general(left, right, (((0,), (0,)), ((), ())), preferred_element_type=F32)


def dot_last(left, right):
    return lax.dot_general(left, right, (((1,), (1,)), ((), ())), preferred_element_type=F32)


def chunk_of(rows):
    return 128 if rows % 128 == 0 else rows


def cost(flops, nbytes):
    return pl.CostEstimate(flops=flops, bytes_accessed=nbytes, transcendentals=0)


def slots_kernel(owners, capacity, routes_ref, slot_ref):
    top, rows = routes_ref.shape
    routes = routes_ref[...]
    expert = lax.broadcasted_iota(jnp.int32, (owners, rows), 0)
    named = [(routes[k : k + 1, :] == expert).astype(F32) for k in range(top)]
    onehot = sum(named)
    before = lax.broadcasted_iota(jnp.int32, (rows, rows), 0) < lax.broadcasted_iota(
        jnp.int32, (rows, rows), 1
    )
    position = dot(onehot.astype(BF), before.astype(F32).astype(BF))
    for k in range(top):
        own = jnp.sum(named[k] * position, axis=0, keepdims=True).astype(jnp.int32)
        slot_ref[k : k + 1, :] = routes[k : k + 1, :] * capacity + own


def select_of(slots, start, count):
    at = lax.broadcasted_iota(jnp.int32, (count, slots.shape[1]), 0) + start
    hit = slots[0:1, :] == at
    for k in range(1, slots.shape[0]):
        hit = hit | (slots[k : k + 1, :] == at)
    return hit


def gather_kernel(chunk, slot_ref, rows_ref, out_ref):
    slots = slot_ref[...]
    for start in range(0, out_ref.shape[0], chunk):
        picked = select_of(slots, start, chunk).astype(F32).astype(BF)
        out_ref[start : start + chunk, :] = dot(picked, rows_ref[...]).astype(BF)


def scaled_kernel(chunk, slot_ref, gates_ref, rows_ref, out_ref):
    slots = slot_ref[...]
    top = slots.shape[0]
    for start in range(0, out_ref.shape[0], chunk):
        at = lax.broadcasted_iota(jnp.int32, (chunk, slots.shape[1]), 0) + start
        weight = jnp.zeros((chunk, slots.shape[1]), F32)
        for k in range(top):
            weight = weight + jnp.where(slots[k : k + 1, :] == at, gates_ref[k : k + 1, :], 0.0)
        picked = select_of(slots, start, chunk).astype(F32).astype(BF)
        gate = jnp.sum(weight, axis=1, keepdims=True)
        out_ref[start : start + chunk, :] = (gate * dot(picked, rows_ref[...])).astype(BF)


def forward_kernel(pieces, at_ref, x_ref, *refs):
    weights = refs[: 3 * pieces]
    out_ref, gate_ref, up_ref, hidden_ref = refs[3 * pieces :]
    width = weights[0].shape[0]
    pre_gate = pre_up = 0.0
    for p in range(pieces):
        cols = pl.ds(pl.multiple_of(at_ref[p], 128), width)
        part = x_ref[:, cols]
        pre_gate = pre_gate + dot(part, weights[p][...])
        pre_up = pre_up + dot(part, weights[pieces + p][...])
    gate_ref[...] = pre_gate
    up_ref[...] = pre_up
    hidden = (pre_gate / (1.0 + jnp.exp(-pre_gate)) * pre_up).astype(BF)
    hidden_ref[...] = hidden
    for p in range(pieces):
        cols = pl.ds(pl.multiple_of(at_ref[p], 128), width)
        out_ref[:, cols] = dot_last(hidden, weights[2 * pieces + p][...]).astype(BF)


def backward_kernel(pieces, at_ref, g_ref, gate_ref, up_ref, *refs):
    weights = refs[: 3 * pieces]
    out_ref, d_gate_ref, d_up_ref = refs[3 * pieces :]
    width = weights[0].shape[0]
    grad = 0.0
    for p in range(pieces):
        cols = pl.ds(pl.multiple_of(at_ref[p], 128), width)
        grad = grad + dot(g_ref[:, cols], weights[2 * pieces + p][...])
    pre_gate = gate_ref[...]
    sig = 1.0 / (1.0 + jnp.exp(-pre_gate))
    d_gate = (grad * up_ref[...] * sig * (1.0 + pre_gate * (1.0 - sig))).astype(BF)
    d_up = (grad * pre_gate * sig).astype(BF)
    d_gate_ref[...] = d_gate
    d_up_ref[...] = d_up
    for p in range(pieces):
        cols = pl.ds(pl.multiple_of(at_ref[p], 128), width)
        out_ref[:, cols] = (
            dot_last(d_gate, weights[p][...]) + dot_last(d_up, weights[pieces + p][...])
        ).astype(BF)


def weights_kernel(width, at_ref, x_ref, g_ref, d_gate_ref, d_up_ref, hidden_ref, out_ref):
    cols = pl.ds(pl.multiple_of(at_ref[pl.program_id(0)], 128), width)
    x = x_ref[:, cols]
    out_ref[0, 0] = dot_rows(x, d_gate_ref[...]).astype(BF)
    out_ref[0, 1] = dot_rows(x, d_up_ref[...]).astype(BF)
    out_ref[0, 2] = dot_rows(g_ref[:, cols], hidden_ref[...]).astype(BF)


def mix_kernel(slot_ref, gates_ref, cot_ref, rows_ref, mixed_ref, grads_ref):
    slots = slot_ref[...]
    rows = rows_ref[...]
    cot = cot_ref[...].astype(F32)
    at = lax.broadcasted_iota(jnp.int32, (rows.shape[0], slots.shape[1]), 0)
    total = 0.0
    for k in range(slots.shape[0]):
        picked = (slots[k : k + 1, :] == at).astype(F32).astype(BF)
        row = dot_rows(picked, rows)
        total = total + gates_ref[:, k : k + 1] * row
        grads_ref[:, k : k + 1] = jnp.sum(cot * row, axis=1, keepdims=True)
    mixed_ref[...] = total.astype(BF)


def combine_kernel(slot_ref, rows_ref, out_ref):
    rows = rows_ref[...]
    picked = select_of(slot_ref[...], 0, rows.shape[0]).astype(F32).astype(BF)
    out_ref[...] = dot_rows(picked, rows).astype(BF)


def whole(shape):
    return pl.BlockSpec(shape, lambda i, *_: (0,) * len(shape))


def expert_call(kernel, at, streamed, weights, outs, chunk, flops):
    rows = streamed[0].shape[0]
    tiles = lambda a: pl.BlockSpec((chunk, a.shape[1]), lambda i, *_: (i, 0))
    nbytes = sum(a.size * a.dtype.itemsize for a in (*streamed, *weights, *outs))
    return pl.pallas_call(
        kernel,
        out_shape=outs,
        grid_spec=pltpu.PrefetchScalarGridSpec(
            num_scalar_prefetch=1,
            grid=(rows // chunk,),
            in_specs=[tiles(a) for a in streamed] + [whole(w.shape) for w in weights],
            out_specs=[tiles(a) for a in outs],
        ),
        cost_estimate=cost(flops, nbytes),
    )(at, *streamed, *weights)


def on_device(tokens, routes, gates, gate_weight, up_weight, down_weight, cotangent):
    owners = lax.axis_size("expert")
    replicas = lax.axis_size("dp")
    tok_rows, feat = tokens.shape
    top = routes.shape[1]
    hid = gate_weight.shape[2]
    pair_count = tok_rows * top
    capacity = max(2, pair_count * 5 // (4 * owners))
    slot_count = owners * capacity
    chunk = chunk_of(slot_count)
    sds = jax.ShapeDtypeStruct

    own = [gate_weight[0], up_weight[0], down_weight[0]]
    share = own[0].shape[0]
    if replicas == 2:
        me = lax.axis_index("dp")
        swap = [(0, 1), (1, 0)]
        peer = [lax.ppermute(w, "dp", swap) for w in own]
        weights = [own[0], peer[0], own[1], peer[1], own[2], peer[2]]
        pieces = 2
        at = jnp.stack([me * share, (1 - me) * share]).astype(jnp.int32)
    else:
        weights = [lax.all_gather(w, "dp", axis=0, tiled=True) for w in own]
        pieces = 1
        at = jnp.zeros((1,), jnp.int32)

    def exchange(rows):
        moved = lax.all_to_all(
            rows.reshape(owners, capacity, feat), "expert", split_axis=0, concat_axis=0, tiled=True
        )
        return moved.reshape(slot_count, feat)

    slots = pl.pallas_call(
        functools.partial(slots_kernel, owners, capacity),
        out_shape=sds((top, tok_rows), jnp.int32),
    )(routes.T)
    row_bytes = slot_count * feat * 2
    picking = cost(2 * slot_count * tok_rows * feat, row_bytes + tok_rows * feat * 2)
    outgoing = pl.pallas_call(
        functools.partial(gather_kernel, chunk),
        out_shape=sds((slot_count, feat), BF),
        cost_estimate=picking,
    )(slots, tokens)
    arrived = exchange(outgoing)
    sendable = pl.pallas_call(
        functools.partial(scaled_kernel, chunk),
        out_shape=sds((slot_count, feat), BF),
        cost_estimate=picking,
    )(slots, gates.T, cotangent)
    arrived_grad = exchange(sendable)

    wide = sds((slot_count, hid), F32)
    narrow = sds((slot_count, hid), BF)
    work = 2 * slot_count * feat * hid
    expert_out, pre_gate, pre_up, hidden = expert_call(
        functools.partial(forward_kernel, pieces),
        at,
        [arrived],
        weights,
        [sds((slot_count, feat), BF), wide, wide, narrow],
        chunk,
        3 * work,
    )
    returned = exchange(expert_out)
    grad_rows, d_gate, d_up = expert_call(
        functools.partial(backward_kernel, pieces),
        at,
        [arrived_grad, pre_gate, pre_up],
        weights,
        [sds((slot_count, feat), BF), narrow, narrow],
        chunk,
        3 * work,
    )
    back_rows = exchange(grad_rows)

    width = feat // pieces
    partial = pl.pallas_call(
        functools.partial(weights_kernel, width),
        out_shape=sds((pieces, 3, width, hid), BF),
        grid_spec=pltpu.PrefetchScalarGridSpec(
            num_scalar_prefetch=1,
            grid=(pieces,),
            in_specs=[whole((slot_count, feat))] * 2 + [whole((slot_count, hid))] * 3,
            out_specs=pl.BlockSpec((1, 3, width, hid), lambda i, *_: (i, 0, 0, 0)),
        ),
        cost_estimate=cost(3 * work, 2 * row_bytes + 12 * feat * hid),
    )(at, arrived, arrived_grad, d_gate, d_up, hidden)
    if replicas == 2:
        got = lax.ppermute(partial[1], "dp", swap)
        grads = [partial[0, i].astype(F32) + got[i].astype(F32) for i in range(3)]
    else:
        got = lax.all_to_all(partial[0], "dp", split_axis=1, concat_axis=0, tiled=True)
        got = got.reshape(replicas, 3, share, hid).astype(F32)
        grads = [jnp.sum(got[:, i], axis=0) for i in range(3)]

    mixed, gate_grads = pl.pallas_call(
        mix_kernel,
        out_shape=(sds((tok_rows, feat), BF), sds((tok_rows, top), F32)),
        cost_estimate=cost(2 * top * slot_count * tok_rows * feat, row_bytes),
    )(slots, gates, cotangent, returned)
    token_grads = pl.pallas_call(
        combine_kernel,
        out_shape=sds((tok_rows, feat), BF),
        cost_estimate=picking,
    )(slots, back_rows)
    return (mixed, token_grads, gate_grads, grads[0][None], grads[1][None], grads[2][None])


def solution(mesh):
    rows = P(("dp", "expert"), None)
    weight = P("expert", "dp", None)
    return jax.shard_map(
        on_device,
        mesh=mesh,
        in_specs=(rows, rows, rows, weight, weight, weight, rows),
        out_specs=(rows, rows, rows, weight, weight, weight),
        check_vma=False,
    )
```

```python
import functools

import jax
import jax.numpy as jnp
from jax import lax
from jax.experimental import pallas as pl
from jax.experimental.pallas import tpu as pltpu
from jax.sharding import PartitionSpec as P

BF = jnp.bfloat16
F32 = jnp.float32


def dot(left, right):
    return jnp.dot(left, right, preferred_element_type=F32)


def dot_rows(left, right):
    return lax.dot_general(left, right, (((0,), (0,)), ((), ())), preferred_element_type=F32)


def dot_last(left, right):
    return lax.dot_general(left, right, (((1,), (1,)), ((), ())), preferred_element_type=F32)


def cost(flops, nbytes):
    return pl.CostEstimate(flops=flops, bytes_accessed=nbytes, transcendentals=0)


def slots_kernel(owners, capacity, routes_ref, gates_ref, out_ref):
    top, rows = routes_ref.shape
    routes = routes_ref[...]
    expert = lax.broadcasted_iota(jnp.int32, (owners, rows), 0)
    named = [(routes[k : k + 1, :] == expert).astype(F32) for k in range(top)]
    onehot = sum(named)
    before = lax.broadcasted_iota(jnp.int32, (rows, rows), 0) < lax.broadcasted_iota(
        jnp.int32, (rows, rows), 1
    )
    position = dot(onehot.astype(BF), before.astype(F32).astype(BF))
    base = (routes * capacity).astype(F32)
    for k in range(top):
        own = jnp.sum(named[k] * position, axis=0, keepdims=True)
        out_ref[k : k + 1, :] = base[k : k + 1, :] + own
    out_ref[top : 2 * top, :] = gates_ref[...]


def slots_of(top, base_ref, plan_ref):
    return plan_ref[0:top, :].astype(jnp.int32) - base_ref[0]


def pick_kernel(chunk, base_ref, plan_ref, tokens_ref, cot_ref, out_ref):
    top = plan_ref.shape[0] // 2
    slots = slots_of(top, base_ref, plan_ref)
    feat = tokens_ref.shape[1]
    for start in range(0, out_ref.shape[0], chunk):
        at = lax.broadcasted_iota(jnp.int32, (chunk, slots.shape[1]), 0) + start
        hits = [slots[k : k + 1, :] == at for k in range(top)]
        weight = sum(
            jnp.where(hit, plan_ref[top + k : top + k + 1, :], 0.0) for k, hit in enumerate(hits)
        )
        gate = jnp.sum(weight, axis=1, keepdims=True)
        picked = sum(hit.astype(F32) for hit in hits).astype(BF)
        rows = slice(start, start + chunk)
        out_ref[rows, :feat] = dot(picked, tokens_ref[...]).astype(BF)
        out_ref[rows, feat:] = (gate * dot(picked, cot_ref[...])).astype(BF)


def expert_kernel(pieces, at_ref, in_ref, *refs):
    weights = refs[: 3 * pieces]
    out_ref, d_gate_ref, d_up_ref, hidden_ref = refs[3 * pieces :]
    feat = in_ref.shape[1] // 2
    width = feat // pieces

    def cols(p, offset):
        return pl.ds(pl.multiple_of(at_ref[p] + offset, 128), width)

    pre_gate = pre_up = grad = 0.0
    for p in range(pieces):
        part = in_ref[:, cols(p, 0)]
        pre_gate = pre_gate + dot(part, weights[p][...])
        pre_up = pre_up + dot(part, weights[pieces + p][...])
    sig = 1.0 / (1.0 + jnp.exp(-pre_gate))
    hidden = (pre_gate * sig * pre_up).astype(BF)
    hidden_ref[...] = hidden
    for p in range(pieces):
        down = weights[2 * pieces + p][...]
        out_ref[:, cols(p, 0)] = dot_last(hidden, down).astype(BF)
        grad = grad + dot(in_ref[:, cols(p, feat)], down)
    d_gate = (grad * pre_up * sig * (1.0 + pre_gate * (1.0 - sig))).astype(BF)
    d_up = (grad * pre_gate * sig).astype(BF)
    d_gate_ref[...] = d_gate
    d_up_ref[...] = d_up
    for p in range(pieces):
        out_ref[:, cols(p, feat)] = (
            dot_last(d_gate, weights[p][...]) + dot_last(d_up, weights[pieces + p][...])
        ).astype(BF)


def weights_kernel(parts, at_ref, *refs):
    ins, out_ref = refs[:-1], refs[-1]
    width = out_ref.shape[1]
    feat = ins[0].shape[1] // 2
    sums = [0.0, 0.0, 0.0]
    for i in range(parts):
        rows, d_gate, d_up, hidden = ins[4 * i : 4 * i + 4]
        x = rows[:, pl.ds(pl.multiple_of(at_ref[0], 128), width)]
        g = rows[:, pl.ds(pl.multiple_of(at_ref[0] + feat, 128), width)]
        sums[0] = sums[0] + dot_rows(x, d_gate[...])
        sums[1] = sums[1] + dot_rows(x, d_up[...])
        sums[2] = sums[2] + dot_rows(g, hidden[...])
    for i in range(3):
        out_ref[i] = sums[i].astype(BF)


def combine_kernel(base_ref, plan_ref, gates_ref, cot_ref, rows_ref, out_ref, grads_ref):
    top = plan_ref.shape[0] // 2
    slots = slots_of(top, base_ref, plan_ref)
    feat = cot_ref.shape[1]
    rows = rows_ref[:, :feat]
    cot = cot_ref[...].astype(F32)
    at = lax.broadcasted_iota(jnp.int32, (rows.shape[0], slots.shape[1]), 0)
    total, every = 0.0, 0.0
    for k in range(top):
        picked = (slots[k : k + 1, :] == at).astype(F32)
        every = every + picked
        row = dot_rows(picked.astype(BF), rows)
        total = total + gates_ref[:, k : k + 1] * row
        grads_ref[:, k : k + 1] = jnp.sum(cot * row, axis=1, keepdims=True)
    out_ref[:, :feat] = total.astype(out_ref.dtype)
    out_ref[:, feat:] = dot_rows(every.astype(BF), rows_ref[:, feat:]).astype(out_ref.dtype)


SMEM = pl.BlockSpec(memory_space=pltpu.SMEM)
VMEM = pl.BlockSpec(memory_space=pltpu.VMEM)


def call(kernel, scalar, arrays, outs, flops):
    one = not isinstance(outs, (list, tuple))
    listed = [outs] if one else list(outs)
    nbytes = sum(a.size * a.dtype.itemsize for a in (*arrays, *listed))
    return pl.pallas_call(
        kernel,
        out_shape=outs,
        in_specs=([] if scalar is None else [SMEM]) + [VMEM] * len(arrays),
        out_specs=VMEM if one else [VMEM] * len(listed),
        cost_estimate=cost(flops, nbytes),
    )(*([] if scalar is None else [scalar]), *arrays)


def on_device(tokens, routes, gates, gate_weight, up_weight, down_weight, cotangent):
    owners = lax.axis_size("expert")
    replicas = lax.axis_size("dp")
    tok_rows, feat = tokens.shape
    top = routes.shape[1]
    hid = gate_weight.shape[2]
    pair_count = tok_rows * top
    capacity = max(2, pair_count * 5 // (4 * owners))
    half = owners // 2
    slot_count = half * capacity
    sds = jax.ShapeDtypeStruct

    across = [(i, (i + half) % owners) for i in range(owners)]
    groups = [list(range(half)), list(range(half, owners))]
    base = ((lax.axis_index("expert") // half) * slot_count).astype(jnp.int32).reshape(1)

    def send(rows):
        return lax.ppermute(rows, "expert", across)

    def exchange(rows):
        moved = lax.all_to_all(
            rows.reshape(half, capacity, 2 * feat),
            "expert",
            split_axis=0,
            concat_axis=0,
            tiled=True,
            axis_index_groups=groups,
        )
        return moved.reshape(slot_count, 2 * feat)

    far_tokens = send(tokens)
    far_cot = send(cotangent)
    plan = call(
        functools.partial(slots_kernel, owners, capacity),
        None,
        [routes.T, gates.T],
        sds((2 * top, tok_rows), F32),
        2 * owners * tok_rows * tok_rows,
    )
    far_plan = send(plan)
    far_gates = send(gates)

    own = [gate_weight[0], up_weight[0], down_weight[0]]
    share = own[0].shape[0]
    if replicas == 2:
        me = lax.axis_index("dp")
        swap = [(0, 1), (1, 0)]
        peer = [lax.ppermute(w, "dp", swap) for w in own]
        weights = [own[0], peer[0], own[1], peer[1], own[2], peer[2]]
        pieces = 2
        at = jnp.stack([me * share, (1 - me) * share]).astype(jnp.int32)
    else:
        weights = [lax.all_gather(w, "dp", axis=0, tiled=True) for w in own]
        pieces = 1
        at = jnp.zeros((1,), jnp.int32)
    width = feat // pieces

    wide = sds((slot_count, 2 * feat), BF)
    narrow = sds((slot_count, hid), BF)
    chunk = 64 if slot_count % 64 == 0 else slot_count
    work = 2 * slot_count * feat * hid

    def pick(plan_at, tokens_at, cot_at):
        return call(
            functools.partial(pick_kernel, chunk),
            base,
            [plan_at, tokens_at, cot_at],
            wide,
            4 * slot_count * tok_rows * feat,
        )

    def expert(rows):
        return call(
            functools.partial(expert_kernel, pieces),
            at,
            [rows, *weights],
            [wide, narrow, narrow, narrow],
            6 * work,
        )

    def combine(plan_at, gates_at, cot_at, rows, dtype):
        return call(
            combine_kernel,
            base,
            [plan_at, gates_at, cot_at, rows],
            [sds((tok_rows, 2 * feat), dtype), sds((tok_rows, top), F32)],
            2 * (top + 1) * slot_count * tok_rows * feat,
        )

    near_in = exchange(pick(plan, tokens, cotangent))
    far_rows = pick(far_plan, far_tokens, far_cot)
    near_in, far_rows = lax.optimization_barrier((near_in, far_rows))
    far_in = exchange(far_rows)
    near_out, *near_parts = expert(near_in)
    far_out, *far_parts = expert(far_in)
    far_back = exchange(far_out)
    near_out, far_back = lax.optimization_barrier((near_out, far_back))
    near_back = exchange(near_out)

    far_sum, far_gg = combine(far_plan, far_gates, far_cot, far_back, BF)
    got_sum = send(far_sum)
    got_gg = send(far_gg)

    def partial(p):
        return call(
            functools.partial(weights_kernel, 2),
            at[p : p + 1],
            [near_in, *near_parts, far_in, *far_parts],
            sds((3, width, hid), BF),
            6 * work // pieces,
        )

    if replicas == 2:
        got = lax.ppermute(partial(1), "dp", swap)
        kept = partial(0)
        grads = [kept[i].astype(F32) + got[i].astype(F32) for i in range(3)]
    else:
        got = lax.all_to_all(partial(0), "dp", split_axis=1, concat_axis=0, tiled=True)
        got = got.reshape(replicas, 3, share, hid).astype(F32)
        grads = [jnp.sum(got[:, i], axis=0) for i in range(3)]

    near_sum, near_gg = combine(plan, gates, cotangent, near_back, F32)
    total = (near_sum + got_sum.astype(F32)).astype(BF)
    mixed, token_grads = total[:, :feat], total[:, feat:]
    gate_grads = near_gg + got_gg
    return (mixed, token_grads, gate_grads, grads[0][None], grads[1][None], grads[2][None])


def solution(mesh):
    rows = P(("dp", "expert"), None)
    weight = P("expert", "dp", None)
    return jax.shard_map(
        on_device,
        mesh=mesh,
        in_specs=(rows, rows, rows, weight, weight, weight, rows),
        out_specs=(rows, rows, rows, weight, weight, weight),
        check_vma=False,
    )
```

```python
import functools

import jax
import jax.numpy as jnp
from jax import lax
from jax.experimental import pallas as pl
from jax.experimental.pallas import tpu as pltpu
from jax.sharding import PartitionSpec as P

BF = jnp.bfloat16
F32 = jnp.float32
STRETCH = 12
NEAR = 0


def dot(left, right):
    return jnp.dot(left, right, preferred_element_type=F32)


def dot_rows(left, right):
    return lax.dot_general(left, right, (((0,), (0,)), ((), ())), preferred_element_type=F32)


def dot_last(left, right):
    return lax.dot_general(left, right, (((1,), (1,)), ((), ())), preferred_element_type=F32)


def cost(flops, nbytes):
    return pl.CostEstimate(flops=flops, bytes_accessed=nbytes, transcendentals=0)


def slots_in(owners, capacity, routes):
    top, rows = routes.shape
    expert = lax.broadcasted_iota(jnp.int32, (owners, rows), 0)
    named = [(routes[k : k + 1, :] == expert).astype(F32) for k in range(top)]
    onehot = sum(named)
    before = lax.broadcasted_iota(jnp.int32, (rows, rows), 0) < lax.broadcasted_iota(
        jnp.int32, (rows, rows), 1
    )
    position = dot(onehot.astype(BF), before.astype(F32).astype(BF)).astype(jnp.int32)
    return [
        routes[k : k + 1, :] * capacity
        + jnp.sum(jnp.where(routes[k : k + 1, :] == expert, position, 0), axis=0, keepdims=True)
        for k in range(top)
    ]


def pick_kernel(owners, capacity, packed, starts_ref, *refs):
    if packed:
        facts_ref, tokens_ref, cot_ref, *outs = refs
        top = facts_ref.shape[0] // 2
        routes = facts_ref[0:top, :].astype(jnp.int32)
        gates = facts_ref[top : 2 * top, :]
    else:
        routes_ref, gates_ref, tokens_ref, cot_ref, *outs = refs
        top = routes_ref.shape[0]
        routes, gates = routes_ref[...], gates_ref[...]
    *outs, plan_ref = outs
    slots = slots_in(owners, capacity, routes)
    for k in range(top):
        plan_ref[k : k + 1, :] = slots[k].astype(F32)
    plan_ref[top : 2 * top, :] = gates
    feat = tokens_ref.shape[1]
    for b, out_ref in enumerate(outs):
        rows = out_ref.shape[0]
        at = lax.broadcasted_iota(jnp.int32, (rows, slots[0].shape[1]), 0) + starts_ref[b]
        hits = [slot == at for slot in slots]
        weight = sum(
            jnp.where(hit, gates[k : k + 1, :], 0.0) for k, hit in enumerate(hits)
        )
        gate = jnp.sum(weight, axis=1, keepdims=True)
        picked = sum(hit.astype(F32) for hit in hits).astype(BF)
        out_ref[:, :feat] = dot(picked, tokens_ref[...]).astype(BF)
        out_ref[:, feat:] = (gate * dot(picked, cot_ref[...])).astype(BF)


def joined(refs, columns):
    if len(refs) == 1:
        return refs[0][:, columns]
    return jnp.concatenate([ref[:, columns] for ref in refs], axis=0)


def store_rows(at_ref, first, out_ref, columns, value):
    if len(out_ref.shape) == 2:
        out_ref[:, columns] = value
        return
    count, rows = out_ref.shape[:2]
    for b in range(count):
        out_ref[at_ref[first + b], :, columns] = value[b * rows : (b + 1) * rows]


def expert_kernel(pieces, blocks, at_ref, *refs):
    ins, weights = refs[:blocks], refs[blocks : blocks + 3 * pieces]
    out_ref, d_gate_ref, d_up_ref, hidden_ref = refs[blocks + 3 * pieces :]
    feat = ins[0].shape[1] // 2
    width = feat // pieces

    def cols(p, offset):
        return pl.ds(pl.multiple_of(at_ref[p] + offset, 128), width)

    pre_gate = pre_up = grad = 0.0
    for p in range(pieces):
        part = joined(ins, cols(p, 0))
        pre_gate = pre_gate + dot(part, weights[p][...])
        pre_up = pre_up + dot(part, weights[pieces + p][...])
    sig = 1.0 / (1.0 + jnp.exp(-pre_gate))
    hidden = (pre_gate * sig * pre_up).astype(BF)
    hidden_ref[...] = hidden
    for p in range(pieces):
        down = weights[2 * pieces + p][...]
        store_rows(at_ref, pieces, out_ref, cols(p, 0), dot_last(hidden, down).astype(BF))
        grad = grad + dot(joined(ins, cols(p, feat)), down)
    d_gate = (grad * pre_up * sig * (1.0 + pre_gate * (1.0 - sig))).astype(BF)
    d_up = (grad * pre_gate * sig).astype(BF)
    d_gate_ref[...] = d_gate
    d_up_ref[...] = d_up
    for p in range(pieces):
        back = dot_last(d_gate, weights[p][...]) + dot_last(d_up, weights[pieces + p][...])
        store_rows(at_ref, pieces, out_ref, cols(p, feat), back.astype(BF))


def weights_kernel(blocks, at_ref, *refs):
    ins, out_ref = refs[:-1], refs[-1]
    width = out_ref.shape[1]
    feat = ins[0].shape[1] // 2
    sums = [0.0, 0.0, 0.0]
    for count in blocks:
        part, ins = ins[: count + 3], ins[count + 3 :]
        rows, (d_gate, d_up, hidden) = part[:count], part[count:]
        x = joined(rows, pl.ds(pl.multiple_of(at_ref[0], 128), width))
        g = joined(rows, pl.ds(pl.multiple_of(at_ref[0] + feat, 128), width))
        sums[0] = sums[0] + dot_rows(x, d_gate[...])
        sums[1] = sums[1] + dot_rows(x, d_up[...])
        sums[2] = sums[2] + dot_rows(g, hidden[...])
    for i in range(3):
        out_ref[i] = sums[i].astype(BF)


def combine_kernel(blocks, starts_ref, plan_ref, cot_ref, *refs):
    ins, (out_ref, grads_ref) = refs[:blocks], refs[blocks:]
    top = plan_ref.shape[0] // 2
    slots = plan_ref[0:top, :].astype(jnp.int32)
    gates = jnp.transpose(plan_ref[...])
    feat = cot_ref.shape[1]
    rows = joined(ins, slice(0, feat))
    cot = cot_ref[...].astype(F32)
    shape = (ins[0].shape[0], slots.shape[1])
    at = [lax.broadcasted_iota(jnp.int32, shape, 0) + starts_ref[b] for b in range(blocks)]
    at = at[0] if blocks == 1 else jnp.concatenate(at, axis=0)
    total, every = 0.0, 0.0
    for k in range(top):
        picked = (slots[k : k + 1, :] == at).astype(F32)
        every = every + picked
        row = dot_rows(picked.astype(BF), rows)
        total = total + gates[:, top + k : top + k + 1] * row
        grads_ref[:, k : k + 1] = jnp.sum(cot * row, axis=1, keepdims=True)
    out_ref[:, :feat] = total.astype(out_ref.dtype)
    back = dot_rows(every.astype(BF), joined(ins, slice(feat, 2 * feat)))
    out_ref[:, feat:] = back.astype(out_ref.dtype)


def finish_kernel(near_ref, far_ref, near_gg_ref, far_gg_ref, mixed_ref, grads_ref, gg_ref):
    feat = mixed_ref.shape[1]
    mixed_ref[...] = (near_ref[:, :feat] + far_ref[:, :feat].astype(F32)).astype(BF)
    grads_ref[...] = (near_ref[:, feat:] + far_ref[:, feat:].astype(F32)).astype(BF)
    gg_ref[...] = near_gg_ref[...] + far_gg_ref[...]


SMEM = pl.BlockSpec(memory_space=pltpu.SMEM)
VMEM = pl.BlockSpec(memory_space=pltpu.VMEM)


def call(kernel, scalar, arrays, outs, flops):
    one = not isinstance(outs, (list, tuple))
    listed = [outs] if one else list(outs)
    nbytes = sum(a.size * a.dtype.itemsize for a in (*arrays, *listed)) if flops else 0
    return pl.pallas_call(
        kernel,
        out_shape=outs,
        in_specs=([] if scalar is None else [SMEM]) + [VMEM] * len(arrays),
        out_specs=VMEM if one else [VMEM] * len(listed),
        cost_estimate=cost(flops, nbytes),
    )(*([] if scalar is None else [scalar]), *arrays)


def on_device(tokens, routes, gates, gate_weight, up_weight, down_weight, cotangent):
    owners = lax.axis_size("expert")
    replicas = lax.axis_size("dp")
    tok_rows, feat = tokens.shape
    top = routes.shape[1]
    hid = gate_weight.shape[2]
    pair_count = tok_rows * top
    capacity = max(2, pair_count * 5 // (4 * owners))
    half = owners // 2
    slot_count = half * capacity
    sds = jax.ShapeDtypeStruct

    group = lax.axis_index("expert") // half
    member = lax.axis_index("expert") % half
    base = group * slot_count
    across = [(i, (i + half) % owners) for i in range(owners)]
    split = half <= 8 and half & (half - 1) == 0
    one_start = base.astype(jnp.int32).reshape(1)
    if split:
        starts = jnp.stack([base + (member ^ k) * capacity for k in range(half)])
        starts = starts.astype(jnp.int32)

    def send(rows):
        return lax.ppermute(rows, "expert", across)

    def exchange(parts):
        if len(parts) > 1:
            moved = [
                lax.ppermute(part, "expert", [(i, i ^ k) for i in range(owners)])
                for k, part in reversed(list(enumerate(parts)))
                if k
            ]
            return [parts[0], *reversed(moved)]
        moved = lax.all_to_all(
            parts[0].reshape(half, capacity, 2 * feat),
            "expert",
            split_axis=0,
            concat_axis=0,
            tiled=True,
            axis_index_groups=[list(range(half)), list(range(half, owners))],
        )
        return [moved.reshape(slot_count, 2 * feat)]

    far_facts = send(jnp.concatenate([routes.T.astype(F32), gates.T], axis=0))
    far_tokens = send(tokens)
    far_cot = send(cotangent)
    own = [gate_weight[0], up_weight[0], down_weight[0]]
    share = own[0].shape[0]
    if replicas == 2:
        me = lax.axis_index("dp")
        swap = [(0, 1), (1, 0)]
        peer = [lax.ppermute(w, "dp", swap) for w in own]
        far_tokens, far_cot, peer[0], peer[1] = lax.optimization_barrier(
            (far_tokens, far_cot, peer[0], peer[1])
        )
        weights = [own[0], peer[0], own[1], peer[1], own[2], peer[2]]
        pieces = 2
        at = jnp.stack([me * share, (1 - me) * share]).astype(jnp.int32)
    else:
        weights = [lax.all_gather(w, "dp", axis=0, tiled=True) for w in own]
        pieces = 1
        at = jnp.zeros((1,), jnp.int32)
    width = feat // pieces

    places = jnp.concatenate([at, (starts - base) // capacity]) if split else at
    whole_rows = [sds((slot_count, 2 * feat), BF)]
    split_rows = [sds((capacity, 2 * feat), BF)] * half if split else whole_rows
    narrow = sds((slot_count, hid), BF)
    work = 2 * slot_count * feat * hid

    def starts_of(rows):
        return starts if len(rows) > 1 else one_start

    def pick(facts, tokens_at, cot_at, rows):
        outs = call(
            functools.partial(pick_kernel, owners, capacity, len(facts) == 1),
            starts_of(rows),
            [*facts, tokens_at, cot_at],
            [*rows, sds((2 * top, tok_rows), F32)],
            4 * slot_count * tok_rows * feat,
        )
        return outs[:-1], outs[-1]

    def expert(rows, stretch):
        outs = call(
            functools.partial(expert_kernel, pieces, len(rows)),
            places,
            [*rows, *weights],
            [sds((half, *rows[0].shape) if len(rows) > 1 else rows[0].shape, BF)] + [narrow] * 3,
            6 * work * stretch,
        )
        return outs[:1], outs[1:]

    def combine(plan_at, cot_at, rows, dtype):
        return call(
            functools.partial(combine_kernel, len(rows)),
            starts_of(rows),
            [plan_at, cot_at, *rows],
            [sds((tok_rows, 2 * feat), dtype), sds((tok_rows, top), F32)],
            2 * (top + 1) * slot_count * tok_rows * feat,
        )

    near_rows, plan = pick((routes.T, gates.T), tokens, cotangent, whole_rows)
    near_in = exchange(near_rows)
    far_rows, far_plan = pick((far_facts,), far_tokens, far_cot, split_rows)
    far_in = exchange(far_rows)
    far_out, far_parts = expert(far_in, STRETCH)
    far_back = exchange(far_out)
    near_out, near_parts = expert(near_in, NEAR)

    def partial(p):
        return call(
            functools.partial(weights_kernel, (len(near_in), len(far_in))),
            at[p : p + 1],
            [*near_in, *near_parts, *far_in, *far_parts],
            sds((3, width, hid), BF),
            6 * work // pieces * NEAR,
        )

    leaving = partial(pieces - 1)
    far_back, leaving = lax.optimization_barrier((far_back, leaving))
    far_sum, far_gg = combine(far_plan, far_cot, far_back, BF)
    near_out, far_sum = lax.optimization_barrier((near_out, far_sum))
    near_back = exchange(near_out)
    got_sum = send(far_sum)
    got_gg = send(far_gg)

    if replicas == 2:
        got = lax.ppermute(leaving, "dp", swap)
        kept = partial(0)
        grads = [kept[i].astype(F32) + got[i].astype(F32) for i in range(3)]
    else:
        got = lax.all_to_all(leaving, "dp", split_axis=1, concat_axis=0, tiled=True)
        got = got.reshape(replicas, 3, share, hid).astype(F32)
        grads = [jnp.sum(got[:, i], axis=0) for i in range(3)]

    near_sum, near_gg = combine(plan, cotangent, near_back, F32)
    mixed, token_grads, gate_grads = call(
        finish_kernel,
        None,
        [near_sum, got_sum, near_gg, got_gg],
        [sds((tok_rows, feat), BF)] * 2 + [sds((tok_rows, top), F32)],
        2 * tok_rows * feat,
    )
    return (mixed, token_grads, gate_grads, grads[0][None], grads[1][None], grads[2][None])


def solution(mesh):
    rows = P(("dp", "expert"), None)
    weight = P("expert", "dp", None)
    return jax.shard_map(
        on_device,
        mesh=mesh,
        in_specs=(rows, rows, rows, weight, weight, weight, rows),
        out_specs=(rows, rows, rows, weight, weight, weight),
        check_vma=False,
    )
```

```python
import functools

import jax
import jax.numpy as jnp
from jax import lax
from jax.experimental import pallas as pl
from jax.experimental.pallas import tpu as pltpu
from jax.sharding import PartitionSpec as P

BF = jnp.bfloat16
F32 = jnp.float32
STRETCH = 12
NEAR = 0


def dot(left, right):
    return jnp.dot(left, right, preferred_element_type=F32)


def dot_rows(left, right):
    return lax.dot_general(left, right, (((0,), (0,)), ((), ())), preferred_element_type=F32)


def dot_last(left, right):
    return lax.dot_general(left, right, (((1,), (1,)), ((), ())), preferred_element_type=F32)


def cost(flops, nbytes):
    return pl.CostEstimate(flops=flops, bytes_accessed=nbytes, transcendentals=0)


def slots_in(owners, capacity, routes):
    top, rows = routes.shape
    expert = lax.broadcasted_iota(jnp.int32, (owners, rows), 0)
    named = [(routes[k : k + 1, :] == expert).astype(F32) for k in range(top)]
    onehot = sum(named)
    before = lax.broadcasted_iota(jnp.int32, (rows, rows), 0) < lax.broadcasted_iota(
        jnp.int32, (rows, rows), 1
    )
    position = dot(onehot.astype(BF), before.astype(F32).astype(BF)).astype(jnp.int32)
    return [
        routes[k : k + 1, :] * capacity
        + jnp.sum(jnp.where(routes[k : k + 1, :] == expert, position, 0), axis=0, keepdims=True)
        for k in range(top)
    ]


def pick_kernel(owners, capacity, packed, starts_ref, *refs):
    if packed:
        facts_ref, tokens_ref, cot_ref, *outs = refs
        top = facts_ref.shape[0] // 2
        routes = facts_ref[0:top, :].astype(jnp.int32)
        gates = facts_ref[top : 2 * top, :]
    else:
        routes_ref, gates_ref, tokens_ref, cot_ref, *outs = refs
        top = routes_ref.shape[0]
        routes, gates = routes_ref[...], gates_ref[...]
    *outs, plan_ref = outs
    slots = slots_in(owners, capacity, routes)
    for k in range(top):
        plan_ref[k : k + 1, :] = slots[k].astype(F32)
    plan_ref[top : 2 * top, :] = gates
    feat = tokens_ref.shape[1]
    for b, out_ref in enumerate(outs):
        rows = out_ref.shape[0]
        at = lax.broadcasted_iota(jnp.int32, (rows, slots[0].shape[1]), 0) + starts_ref[b]
        hits = [slot == at for slot in slots]
        weight = sum(
            jnp.where(hit, gates[k : k + 1, :], 0.0) for k, hit in enumerate(hits)
        )
        gate = jnp.sum(weight, axis=1, keepdims=True)
        picked = sum(hit.astype(F32) for hit in hits).astype(BF)
        out_ref[:, :feat] = dot(picked, tokens_ref[...]).astype(BF)
        out_ref[:, feat:] = (gate * dot(picked, cot_ref[...])).astype(BF)


def joined(refs, columns):
    if len(refs) == 1:
        return refs[0][:, columns]
    return jnp.concatenate([ref[:, columns] for ref in refs], axis=0)


def store_rows(at_ref, first, out_ref, columns, value):
    if len(out_ref.shape) == 2:
        out_ref[:, columns] = value
        return
    count, rows = out_ref.shape[:2]
    for b in range(count):
        out_ref[at_ref[first + b], :, columns] = value[b * rows : (b + 1) * rows]


def expert_kernel(pieces, blocks, at_ref, *refs):
    ins, weights = refs[:blocks], refs[blocks : blocks + 3 * pieces]
    out_ref, d_gate_ref, d_up_ref, hidden_ref = refs[blocks + 3 * pieces :]
    feat = ins[0].shape[1] // 2
    width = feat // pieces

    def cols(p, offset):
        return pl.ds(pl.multiple_of(at_ref[p] + offset, 128), width)

    pre_gate = pre_up = grad = 0.0
    for p in range(pieces):
        part = joined(ins, cols(p, 0))
        pre_gate = pre_gate + dot(part, weights[p][...])
        pre_up = pre_up + dot(part, weights[pieces + p][...])
    sig = 1.0 / (1.0 + jnp.exp(-pre_gate))
    hidden = (pre_gate * sig * pre_up).astype(BF)
    hidden_ref[...] = hidden
    for p in range(pieces):
        down = weights[2 * pieces + p][...]
        store_rows(at_ref, pieces, out_ref, cols(p, 0), dot_last(hidden, down).astype(BF))
        grad = grad + dot(joined(ins, cols(p, feat)), down)
    d_gate = (grad * pre_up * sig * (1.0 + pre_gate * (1.0 - sig))).astype(BF)
    d_up = (grad * pre_gate * sig).astype(BF)
    d_gate_ref[...] = d_gate
    d_up_ref[...] = d_up
    for p in range(pieces):
        back = dot_last(d_gate, weights[p][...]) + dot_last(d_up, weights[pieces + p][...])
        store_rows(at_ref, pieces, out_ref, cols(p, feat), back.astype(BF))


def weights_kernel(blocks, pieces, at_ref, *refs):
    ins, outs = refs[:-pieces], refs[-pieces:]
    width = outs[0].shape[1]
    feat = ins[0].shape[1] // 2
    for p in range(pieces):
        sums = [0.0, 0.0, 0.0]
        rest = ins
        for count in blocks:
            part, rest = rest[: count + 3], rest[count + 3 :]
            rows, (d_gate, d_up, hidden) = part[:count], part[count:]
            x = joined(rows, pl.ds(pl.multiple_of(at_ref[p], 128), width))
            g = joined(rows, pl.ds(pl.multiple_of(at_ref[p] + feat, 128), width))
            sums[0] = sums[0] + dot_rows(x, d_gate[...])
            sums[1] = sums[1] + dot_rows(x, d_up[...])
            sums[2] = sums[2] + dot_rows(g, hidden[...])
        for i in range(3):
            outs[p][i] = sums[i].astype(BF)


def add_kernel(kept_ref, got_ref, *outs):
    for i, out_ref in enumerate(outs):
        out_ref[0] = kept_ref[i].astype(F32) + got_ref[i].astype(F32)


def combine_kernel(blocks, starts_ref, plan_ref, cot_ref, *refs):
    ins, (out_ref, grads_ref) = refs[:blocks], refs[blocks:]
    top = plan_ref.shape[0] // 2
    slots = plan_ref[0:top, :].astype(jnp.int32)
    gates = jnp.transpose(plan_ref[...])
    feat = cot_ref.shape[1]
    rows = joined(ins, slice(0, feat))
    cot = cot_ref[...].astype(F32)
    shape = (ins[0].shape[0], slots.shape[1])
    at = [lax.broadcasted_iota(jnp.int32, shape, 0) + starts_ref[b] for b in range(blocks)]
    at = at[0] if blocks == 1 else jnp.concatenate(at, axis=0)
    total, every = 0.0, 0.0
    lane = lax.broadcasted_iota(jnp.int32, (slots.shape[1], 128), 1)
    grads = jnp.zeros((slots.shape[1], 128), F32)
    for k in range(top):
        picked = (slots[k : k + 1, :] == at).astype(F32)
        every = every + picked
        row = dot_rows(picked.astype(BF), rows)
        total = total + gates[:, top + k : top + k + 1] * row
        grads = jnp.where(lane == k, jnp.sum(cot * row, axis=1, keepdims=True), grads)
    grads_ref[...] = jnp.transpose(grads)[0 : grads_ref.shape[0], :]
    out_ref[:, :feat] = total.astype(out_ref.dtype)
    back = dot_rows(every.astype(BF), joined(ins, slice(feat, 2 * feat)))
    out_ref[:, feat:] = back.astype(out_ref.dtype)


def finish_kernel(near_ref, far_ref, near_gg_ref, far_gg_ref, mixed_ref, grads_ref, gg_ref):
    feat = mixed_ref.shape[1]
    mixed_ref[...] = (near_ref[:, :feat] + far_ref[:, :feat].astype(F32)).astype(BF)
    grads_ref[...] = (near_ref[:, feat:] + far_ref[:, feat:].astype(F32)).astype(BF)
    gg_ref[...] = (near_gg_ref[...] + far_gg_ref[...])[0 : gg_ref.shape[0], :]


SMEM = pl.BlockSpec(memory_space=pltpu.SMEM)
VMEM = pl.BlockSpec(memory_space=pltpu.VMEM)


def near(value):
    return pltpu.with_memory_space_constraint(value, pltpu.VMEM)


def far(value):
    return pltpu.with_memory_space_constraint(value, pltpu.HBM)


def call(kernel, scalar, arrays, outs, flops):
    nbytes = sum(a.size * a.dtype.itemsize for a in arrays) if flops else 0
    return pl.pallas_call(
        kernel,
        out_shape=outs,
        in_specs=([] if scalar is None else [SMEM]) + [VMEM] * len(arrays),
        out_specs=[VMEM] * len(outs),
        compiler_params=pltpu.CompilerParams(vmem_limit_bytes=16 << 20),
        cost_estimate=cost(flops, nbytes),
    )(*([] if scalar is None else [scalar]), *arrays)


def on_device(tokens, routes, gates, gate_weight, up_weight, down_weight, cotangent):
    owners = lax.axis_size("expert")
    replicas = lax.axis_size("dp")
    tok_rows, feat = tokens.shape
    top = routes.shape[1]
    hid = gate_weight.shape[2]
    pair_count = tok_rows * top
    capacity = max(2, pair_count * 5 // (4 * owners))
    half = owners // 2
    slot_count = half * capacity
    sds = jax.ShapeDtypeStruct

    group = lax.axis_index("expert") // half
    member = lax.axis_index("expert") % half
    base = group * slot_count
    across = [(i, (i + half) % owners) for i in range(owners)]
    split = half <= 8 and half & (half - 1) == 0
    one_start = base.astype(jnp.int32).reshape(1)
    if split:
        starts = jnp.stack([base + (member ^ k) * capacity for k in range(half)])
        starts = starts.astype(jnp.int32)

    def send(rows):
        return lax.ppermute(rows, "expert", across)

    def exchange(parts):
        if len(parts) > 1:
            moved = [
                lax.ppermute(part, "expert", [(i, i ^ k) for i in range(owners)])
                for k, part in reversed(list(enumerate(parts)))
                if k
            ]
            return [parts[0], *reversed(moved)]
        moved = lax.all_to_all(
            parts[0].reshape(half, capacity, 2 * feat),
            "expert",
            split_axis=0,
            concat_axis=0,
            tiled=True,
            axis_index_groups=[list(range(half)), list(range(half, owners))],
        )
        return [moved.reshape(slot_count, 2 * feat)]

    far_facts = send(jnp.concatenate([routes.T.astype(F32), gates.T], axis=0))
    far_tokens = send(tokens)
    far_cot = send(cotangent)
    own = [gate_weight[0], up_weight[0], down_weight[0]]
    share = own[0].shape[0]
    if replicas == 2:
        me = lax.axis_index("dp")
        swap = [(0, 1), (1, 0)]
        peer = [lax.ppermute(w, "dp", swap) for w in own]
        far_tokens, far_cot, peer[0], peer[1] = lax.optimization_barrier(
            (far_tokens, far_cot, peer[0], peer[1])
        )
        weights = [own[0], peer[0], own[1], peer[1], own[2], peer[2]]
        pieces = 2
        at = jnp.stack([me * share, (1 - me) * share]).astype(jnp.int32)
    else:
        weights = [lax.all_gather(w, "dp", axis=0, tiled=True) for w in own]
        pieces = 1
        at = jnp.zeros((1,), jnp.int32)
    width = feat // pieces

    places = jnp.concatenate([at, (starts - base) // capacity]) if split else at
    whole_rows = [pltpu.VMEM((slot_count, 2 * feat), BF)]
    split_rows = whole_rows
    if split:
        split_rows = [pltpu.HBM((capacity, 2 * feat), BF)]
        split_rows = split_rows + [pltpu.VMEM((capacity, 2 * feat), BF)] * (half - 1)
    narrow = pltpu.HBM((slot_count, hid), BF)
    first_weights = [far(w) if i % pieces == 0 else near(w) for i, w in enumerate(weights)]
    weights = [far(w) for w in weights]
    plan_like = sds((2 * top, tok_rows), F32)
    work = 2 * slot_count * feat * hid

    def starts_of(rows):
        return starts if len(rows) > 1 else one_start

    def pick(facts, tokens_at, cot_at, rows):
        outs = call(
            functools.partial(pick_kernel, owners, capacity, len(facts) == 1),
            starts_of(rows),
            [*facts, tokens_at, cot_at],
            [*rows, plan_like],
            4 * slot_count * tok_rows * feat,
        )
        return outs[:-1], outs[-1]

    def expert(rows, weights_at, stretch):
        shape = (half, *rows[0].shape) if len(rows) > 1 else rows[0].shape
        outs = call(
            functools.partial(expert_kernel, pieces, len(rows)),
            places,
            [*[near(r) for r in rows], *weights_at],
            [pltpu.VMEM(shape, BF)] + [narrow] * 3,
            6 * work * stretch,
        )
        return outs[:1], outs[1:]

    def combine(plan_at, cot_at, rows, dtype, space):
        return call(
            functools.partial(combine_kernel, len(rows)),
            starts_of(rows),
            [plan_at, cot_at, *[near(r) for r in rows]],
            [space((tok_rows, 2 * feat), dtype), pltpu.VMEM((8, tok_rows), F32)],
            2 * (top + 1) * slot_count * tok_rows * feat,
        )

    near_rows, plan = pick(
        (far(routes.T), far(gates.T)), far(tokens), far(cotangent), whole_rows
    )
    near_in = exchange(near_rows)
    far_rows, far_plan = pick((near(far_facts),), near(far_tokens), near(far_cot), split_rows)
    far_in = exchange(far_rows)
    far_out, far_parts = expert(far_in, first_weights, STRETCH)
    far_back = exchange(far_out)
    near_out, near_parts = expert(near_in, weights, NEAR)

    partials = call(
        functools.partial(weights_kernel, (len(near_in), len(far_in)), pieces),
        at,
        [far(x) for x in (*near_in, *near_parts, *far_in, *far_parts)],
        [pltpu.HBM((3, width, hid), BF)] * pieces,
        6 * work * NEAR,
    )
    leaving = partials[-1]
    far_back, leaving = lax.optimization_barrier((far_back, leaving))
    far_sum, far_gg = combine(far_plan, far(far_cot), far_back, BF, pltpu.HBM)
    near_out, far_sum = lax.optimization_barrier((near_out, far_sum))
    near_back = exchange(near_out)
    got_sum = send(far_sum)
    got_gg = send(far_gg)

    if replicas == 2:
        got = lax.ppermute(leaving, "dp", swap)
        grads = call(
            add_kernel,
            None,
            [far(partials[0]), near(got)],
            [sds((1, share, hid), F32)] * 3,
            6 * work * STRETCH,
        )
    else:
        got = lax.all_to_all(leaving, "dp", split_axis=1, concat_axis=0, tiled=True)
        got = got.reshape(replicas, 3, share, hid).astype(F32)
        grads = [jnp.sum(got[:, i], axis=0)[None] for i in range(3)]

    near_sum, near_gg = combine(plan, far(cotangent), near_back, F32, pltpu.VMEM)
    mixed, token_grads, gate_grads = call(
        finish_kernel,
        None,
        [near(near_sum), near(got_sum), near(near_gg), near(got_gg)],
        [sds((tok_rows, feat), BF)] * 2 + [sds((top, tok_rows), F32)],
        2 * tok_rows * feat,
    )
    return (mixed, token_grads, gate_grads.T, *grads)


def solution(mesh):
    rows = P(("dp", "expert"), None)
    weight = P("expert", "dp", None)
    return jax.shard_map(
        on_device,
        mesh=mesh,
        in_specs=(rows, rows, rows, weight, weight, weight, rows),
        out_specs=(rows, rows, rows, weight, weight, weight),
        check_vma=False,
    )
```

```python
import functools

import jax
import jax.numpy as jnp
from jax import lax
from jax.experimental import pallas as pl
from jax.experimental.pallas import tpu as pltpu
from jax.sharding import PartitionSpec as P

BF = jnp.bfloat16
F32 = jnp.float32
STRETCH = 12
NEAR = 0
PICK = 12
EARLY = 0
LATE = 12


def dot(left, right):
    return jnp.dot(left, right, preferred_element_type=F32)


def dot_rows(left, right):
    return lax.dot_general(left, right, (((0,), (0,)), ((), ())), preferred_element_type=F32)


def dot_last(left, right):
    return lax.dot_general(left, right, (((1,), (1,)), ((), ())), preferred_element_type=F32)


def cost(flops, nbytes):
    return pl.CostEstimate(flops=flops, bytes_accessed=nbytes, transcendentals=0)


def slots_in(owners, capacity, routes):
    top, rows = routes.shape
    expert = lax.broadcasted_iota(jnp.int32, (owners, rows), 0)
    named = [(routes[k : k + 1, :] == expert).astype(F32) for k in range(top)]
    onehot = sum(named)
    before = lax.broadcasted_iota(jnp.int32, (rows, rows), 0) < lax.broadcasted_iota(
        jnp.int32, (rows, rows), 1
    )
    position = dot(onehot.astype(BF), before.astype(F32).astype(BF)).astype(jnp.int32)
    return [
        routes[k : k + 1, :] * capacity
        + jnp.sum(jnp.where(routes[k : k + 1, :] == expert, position, 0), axis=0, keepdims=True)
        for k in range(top)
    ]


def pick_kernel(owners, capacity, packed, starts_ref, *refs):
    if packed:
        facts_ref, tokens_ref, cot_ref, *outs = refs
        top = facts_ref.shape[0] // 2
        routes = facts_ref[0:top, :].astype(jnp.int32)
        gates = facts_ref[top : 2 * top, :]
    else:
        routes_ref, gates_ref, tokens_ref, cot_ref, *outs = refs
        top = routes_ref.shape[0]
        routes, gates = routes_ref[...], gates_ref[...]
    *outs, plan_ref = outs
    slots = slots_in(owners, capacity, routes)
    for k in range(top):
        plan_ref[k : k + 1, :] = slots[k].astype(F32)
    plan_ref[top : 2 * top, :] = gates
    feat = tokens_ref.shape[1]
    for b, out_ref in enumerate(outs):
        rows = out_ref.shape[0]
        at = lax.broadcasted_iota(jnp.int32, (rows, slots[0].shape[1]), 0) + starts_ref[b]
        hits = [slot == at for slot in slots]
        weight = sum(
            jnp.where(hit, gates[k : k + 1, :], 0.0) for k, hit in enumerate(hits)
        )
        gate = jnp.sum(weight, axis=1, keepdims=True)
        picked = sum(hit.astype(F32) for hit in hits).astype(BF)
        out_ref[:, :feat] = dot(picked, tokens_ref[...]).astype(BF)
        out_ref[:, feat:] = (gate * dot(picked, cot_ref[...])).astype(BF)


def joined(refs, columns):
    if len(refs) == 1:
        return refs[0][:, columns]
    return jnp.concatenate([ref[:, columns] for ref in refs], axis=0)


def store_rows(at_ref, first, out_ref, columns, value):
    if len(out_ref.shape) == 2:
        out_ref[:, columns] = value
        return
    count, rows = out_ref.shape[:2]
    for b in range(count):
        out_ref[at_ref[first + b], :, columns] = value[b * rows : (b + 1) * rows]


def expert_kernel(pieces, blocks, at_ref, *refs):
    ins, weights = refs[:blocks], refs[blocks : blocks + 3 * pieces]
    out_ref, d_gate_ref, d_up_ref, hidden_ref = refs[blocks + 3 * pieces :]
    feat = ins[0].shape[1] // 2
    width = feat // pieces

    def cols(p, offset):
        return pl.ds(pl.multiple_of(at_ref[p] + offset, 128), width)

    pre_gate = pre_up = grad = 0.0
    for p in range(pieces):
        part = joined(ins, cols(p, 0))
        pre_gate = pre_gate + dot(part, weights[p][...])
        pre_up = pre_up + dot(part, weights[pieces + p][...])
    sig = 1.0 / (1.0 + jnp.exp(-pre_gate))
    hidden = (pre_gate * sig * pre_up).astype(BF)
    hidden_ref[...] = hidden
    for p in range(pieces):
        down = weights[2 * pieces + p][...]
        store_rows(at_ref, pieces, out_ref, cols(p, 0), dot_last(hidden, down).astype(BF))
        grad = grad + dot(joined(ins, cols(p, feat)), down)
    d_gate = (grad * pre_up * sig * (1.0 + pre_gate * (1.0 - sig))).astype(BF)
    d_up = (grad * pre_gate * sig).astype(BF)
    d_gate_ref[...] = d_gate
    d_up_ref[...] = d_up
    for p in range(pieces):
        back = dot_last(d_gate, weights[p][...]) + dot_last(d_up, weights[pieces + p][...])
        store_rows(at_ref, pieces, out_ref, cols(p, feat), back.astype(BF))


def weights_kernel(blocks, pieces, at_ref, *refs):
    ins, outs = refs[:-pieces], refs[-pieces:]
    width = outs[0].shape[1]
    feat = ins[0].shape[1] // 2
    for p in range(pieces):
        sums = [0.0, 0.0, 0.0]
        rest = ins
        for count in blocks:
            part, rest = rest[: count + 3], rest[count + 3 :]
            rows, (d_gate, d_up, hidden) = part[:count], part[count:]
            x = joined(rows, pl.ds(pl.multiple_of(at_ref[p], 128), width))
            g = joined(rows, pl.ds(pl.multiple_of(at_ref[p] + feat, 128), width))
            sums[0] = sums[0] + dot_rows(x, d_gate[...])
            sums[1] = sums[1] + dot_rows(x, d_up[...])
            sums[2] = sums[2] + dot_rows(g, hidden[...])
        for i in range(3):
            outs[p][i] = sums[i].astype(BF)


def add_kernel(kept_ref, got_ref, *outs):
    for i, out_ref in enumerate(outs):
        out_ref[0] = kept_ref[i].astype(F32) + got_ref[i].astype(F32)


def combine_kernel(blocks, starts_ref, plan_ref, cot_ref, *refs):
    ins, (out_ref, grads_ref) = refs[:blocks], refs[blocks:]
    top = plan_ref.shape[0] // 2
    slots = plan_ref[0:top, :].astype(jnp.int32)
    gates = jnp.transpose(plan_ref[...])
    feat = cot_ref.shape[1]
    rows = joined(ins, slice(0, feat))
    cot = cot_ref[...].astype(F32)
    shape = (ins[0].shape[0], slots.shape[1])
    at = [lax.broadcasted_iota(jnp.int32, shape, 0) + starts_ref[b] for b in range(blocks)]
    at = at[0] if blocks == 1 else jnp.concatenate(at, axis=0)
    total, every = 0.0, 0.0
    lane = lax.broadcasted_iota(jnp.int32, (slots.shape[1], 128), 1)
    grads = jnp.zeros((slots.shape[1], 128), F32)
    for k in range(top):
        picked = (slots[k : k + 1, :] == at).astype(F32)
        every = every + picked
        row = dot_rows(picked.astype(BF), rows)
        total = total + gates[:, top + k : top + k + 1] * row
        grads = jnp.where(lane == k, jnp.sum(cot * row, axis=1, keepdims=True), grads)
    grads_ref[...] = jnp.transpose(grads)[0 : grads_ref.shape[0], :]
    out_ref[:, :feat] = total.astype(out_ref.dtype)
    back = dot_rows(every.astype(BF), joined(ins, slice(feat, 2 * feat)))
    out_ref[:, feat:] = back.astype(out_ref.dtype)


def finish_kernel(near_ref, far_ref, near_gg_ref, far_gg_ref, mixed_ref, grads_ref, gg_ref):
    feat = mixed_ref.shape[1]
    mixed_ref[...] = (near_ref[:, :feat] + far_ref[:, :feat].astype(F32)).astype(BF)
    grads_ref[...] = (near_ref[:, feat:] + far_ref[:, feat:].astype(F32)).astype(BF)
    gg_ref[...] = (near_gg_ref[...] + far_gg_ref[...])[0 : gg_ref.shape[0], :]


SMEM = pl.BlockSpec(memory_space=pltpu.SMEM)
VMEM = pl.BlockSpec(memory_space=pltpu.VMEM)


def near(value):
    return pltpu.with_memory_space_constraint(value, pltpu.VMEM)


def far(value):
    return pltpu.with_memory_space_constraint(value, pltpu.HBM)


def call(kernel, scalar, arrays, outs, flops):
    nbytes = sum(a.size * a.dtype.itemsize for a in arrays) if flops else 0
    return pl.pallas_call(
        kernel,
        out_shape=outs,
        in_specs=([] if scalar is None else [SMEM]) + [VMEM] * len(arrays),
        out_specs=[VMEM] * len(outs),
        compiler_params=pltpu.CompilerParams(vmem_limit_bytes=16 << 20),
        cost_estimate=cost(flops, nbytes),
    )(*([] if scalar is None else [scalar]), *arrays)


def on_device(tokens, routes, gates, gate_weight, up_weight, down_weight, cotangent):
    owners = lax.axis_size("expert")
    replicas = lax.axis_size("dp")
    tok_rows, feat = tokens.shape
    top = routes.shape[1]
    hid = gate_weight.shape[2]
    pair_count = tok_rows * top
    capacity = max(2, pair_count * 5 // (4 * owners))
    half = owners // 2
    slot_count = half * capacity
    sds = jax.ShapeDtypeStruct

    group = lax.axis_index("expert") // half
    member = lax.axis_index("expert") % half
    base = group * slot_count
    across = [(i, (i + half) % owners) for i in range(owners)]
    split = half <= 8 and half & (half - 1) == 0
    one_start = base.astype(jnp.int32).reshape(1)
    if split:
        starts = jnp.stack([base + (member ^ k) * capacity for k in range(half)])
        starts = starts.astype(jnp.int32)

    def send(rows):
        return lax.ppermute(rows, "expert", across)

    def exchange(parts):
        if len(parts) > 1:
            moved = [
                lax.ppermute(part, "expert", [(i, i ^ k) for i in range(owners)])
                for k, part in reversed(list(enumerate(parts)))
                if k
            ]
            return [parts[0], *reversed(moved)]
        moved = lax.all_to_all(
            parts[0].reshape(half, capacity, 2 * feat),
            "expert",
            split_axis=0,
            concat_axis=0,
            tiled=True,
            axis_index_groups=[list(range(half)), list(range(half, owners))],
        )
        return [moved.reshape(slot_count, 2 * feat)]

    far_facts = send(jnp.concatenate([routes.T.astype(F32), gates.T], axis=0))
    far_tokens = send(tokens)
    far_cot = send(cotangent)
    own = [gate_weight[0], up_weight[0], down_weight[0]]
    share = own[0].shape[0]
    if replicas == 2:
        me = lax.axis_index("dp")
        swap = [(0, 1), (1, 0)]
        peer = [lax.ppermute(w, "dp", swap) for w in own]
        far_tokens, far_cot, peer[0], peer[1] = lax.optimization_barrier(
            (far_tokens, far_cot, peer[0], peer[1])
        )
        weights = [own[0], peer[0], own[1], peer[1], own[2], peer[2]]
        pieces = 2
        at = jnp.stack([me * share, (1 - me) * share]).astype(jnp.int32)
    else:
        weights = [lax.all_gather(w, "dp", axis=0, tiled=True) for w in own]
        pieces = 1
        at = jnp.zeros((1,), jnp.int32)
    width = feat // pieces

    places = jnp.concatenate([at, (starts - base) // capacity]) if split else at
    whole_rows = [pltpu.VMEM((slot_count, 2 * feat), BF)]
    split_rows = whole_rows
    if split:
        split_rows = [pltpu.HBM((capacity, 2 * feat), BF)]
        split_rows = split_rows + [pltpu.VMEM((capacity, 2 * feat), BF)] * (half - 1)
    narrow = pltpu.HBM((slot_count, hid), BF)
    first_weights = [far(w) if i % pieces == 0 else near(w) for i, w in enumerate(weights)]
    weights = [far(w) for w in weights]
    plan_like = sds((2 * top, tok_rows), F32)
    work = 2 * slot_count * feat * hid

    def starts_of(rows):
        return starts if len(rows) > 1 else one_start

    def pick(facts, tokens_at, cot_at, rows, stretch):
        outs = call(
            functools.partial(pick_kernel, owners, capacity, len(facts) == 1),
            starts_of(rows),
            [*facts, tokens_at, cot_at],
            [*rows, plan_like],
            6 * work * stretch,
        )
        return outs[:-1], outs[-1]

    def expert(rows, weights_at, stretch):
        shape = (half, *rows[0].shape) if len(rows) > 1 else rows[0].shape
        outs = call(
            functools.partial(expert_kernel, pieces, len(rows)),
            places,
            [*[near(r) for r in rows], *weights_at],
            [pltpu.VMEM(shape, BF)] + [narrow] * 3,
            6 * work * stretch,
        )
        return outs[:1], outs[1:]

    def combine(plan_at, cot_at, rows, dtype, space):
        return call(
            functools.partial(combine_kernel, len(rows)),
            starts_of(rows),
            [plan_at, cot_at, *[near(r) for r in rows]],
            [space((tok_rows, 2 * feat), dtype), pltpu.VMEM((8, tok_rows), F32)],
            6 * work * NEAR,
        )

    near_rows, plan = pick(
        (far(routes.T), far(gates.T)), far(tokens), far(cotangent), whole_rows, NEAR
    )
    near_in = exchange(near_rows)
    far_rows, far_plan = pick((near(far_facts),), near(far_tokens), near(far_cot), split_rows, PICK)
    far_in = exchange(far_rows)
    near_out, near_parts = expert(near_in, first_weights, EARLY)
    far_in[0], near_parts = lax.optimization_barrier((far_in[0], near_parts))
    far_out, far_parts = expert(far_in, weights, STRETCH)
    far_back = exchange(far_out)

    partials = call(
        functools.partial(weights_kernel, (len(near_in), len(far_in)), pieces),
        at,
        [far(x) for x in (*near_in, *near_parts, *far_in, *far_parts)],
        [pltpu.HBM((3, width, hid), BF)] * pieces,
        6 * work * NEAR,
    )
    leaving = partials[-1]
    far_back, leaving, near_out = lax.optimization_barrier((far_back, leaving, near_out))
    near_back = exchange(near_out)
    far_sum, far_gg = combine(far_plan, far(far_cot), far_back, BF, pltpu.HBM)
    got_sum = send(far_sum)
    got_gg = send(far_gg)

    if replicas == 2:
        got = lax.ppermute(leaving, "dp", swap)
        grads = call(
            add_kernel,
            None,
            [far(partials[0]), near(got)],
            [sds((1, share, hid), F32)] * 3,
            6 * work * LATE,
        )
    else:
        got = lax.all_to_all(leaving, "dp", split_axis=1, concat_axis=0, tiled=True)
        got = got.reshape(replicas, 3, share, hid).astype(F32)
        grads = [jnp.sum(got[:, i], axis=0)[None] for i in range(3)]

    near_sum, near_gg = combine(plan, far(cotangent), near_back, F32, pltpu.VMEM)
    mixed, token_grads, gate_grads = call(
        finish_kernel,
        None,
        [near(near_sum), near(got_sum), near(near_gg), near(got_gg)],
        [sds((tok_rows, feat), BF)] * 2 + [sds((top, tok_rows), F32)],
        2 * tok_rows * feat,
    )
    return (mixed, token_grads, gate_grads.T, *grads)


def solution(mesh):
    rows = P(("dp", "expert"), None)
    weight = P("expert", "dp", None)
    return jax.shard_map(
        on_device,
        mesh=mesh,
        in_specs=(rows, rows, rows, weight, weight, weight, rows),
        out_specs=(rows, rows, rows, weight, weight, weight),
        check_vma=False,
    )
```

```python
import functools

import jax
import jax.numpy as jnp
from jax import lax
from jax.experimental import pallas as pl
from jax.experimental.pallas import tpu as pltpu
from jax.sharding import PartitionSpec as P

BF = jnp.bfloat16
F32 = jnp.float32
STRETCH = 12
NEAR = 0
PICK = 12
EARLY = 0
LATE = 12


def dot(left, right):
    return jnp.dot(left, right, preferred_element_type=F32)


def dot_rows(left, right):
    return lax.dot_general(left, right, (((0,), (0,)), ((), ())), preferred_element_type=F32)


def dot_last(left, right):
    return lax.dot_general(left, right, (((1,), (1,)), ((), ())), preferred_element_type=F32)


def cost(flops, nbytes):
    return pl.CostEstimate(flops=flops, bytes_accessed=nbytes, transcendentals=0)


def slots_in(owners, capacity, routes):
    top, rows = routes.shape
    expert = lax.broadcasted_iota(jnp.int32, (owners, rows), 0)
    named = [(routes[k : k + 1, :] == expert).astype(F32) for k in range(top)]
    onehot = sum(named)
    before = lax.broadcasted_iota(jnp.int32, (rows, rows), 0) < lax.broadcasted_iota(
        jnp.int32, (rows, rows), 1
    )
    position = dot(onehot.astype(BF), before.astype(F32).astype(BF)).astype(jnp.int32)
    return [
        routes[k : k + 1, :] * capacity
        + jnp.sum(jnp.where(routes[k : k + 1, :] == expert, position, 0), axis=0, keepdims=True)
        for k in range(top)
    ]


def pick_kernel(owners, capacity, packed, starts_ref, *refs):
    if packed:
        parcel_ref, rest_ref, cot_ref, *outs, plan_ref = refs
        top = plan_ref.shape[0] // 2
        rows, first = cot_ref.shape[0], cot_ref.shape[0] // 2
        facts = parcel_ref[first : first + 4 * top, 0:rows].astype(F32)
        routes = facts[0:top, :].astype(jnp.int32)
        gates = facts[top : 2 * top] + facts[2 * top : 3 * top] + facts[3 * top : 4 * top]
        tokens = jnp.concatenate([parcel_ref[0:first, :], rest_ref[...]], axis=0)
    else:
        routes_ref, gates_ref, tokens_ref, cot_ref, *outs, plan_ref, parcel_ref, rest_ref = refs
        top = plan_ref.shape[0] // 2
        rows, first = cot_ref.shape[0], cot_ref.shape[0] // 2
        routes, gates, tokens = routes_ref[...], gates_ref[...], tokens_ref[...]
        high = gates.astype(BF)
        after = gates - high.astype(F32)
        middle = after.astype(BF)
        low = after - middle.astype(F32)
        facts = [routes.astype(F32), high.astype(F32), middle.astype(F32), low]
        parcel_ref[0:first, :] = tokens[:first]
        rest_ref[...] = tokens[first:]
        parcel_ref[first : first + 4 * top, :] = jnp.zeros((4 * top, tokens.shape[1]), BF)
        parcel_ref[first : first + 4 * top, 0:rows] = jnp.concatenate(facts, axis=0).astype(BF)
    slots = slots_in(owners, capacity, routes)
    for k in range(top):
        plan_ref[k : k + 1, :] = slots[k].astype(F32)
    plan_ref[top : 2 * top, :] = gates
    feat = tokens.shape[1]
    for b, out_ref in enumerate(outs):
        rows = out_ref.shape[0]
        at = lax.broadcasted_iota(jnp.int32, (rows, slots[0].shape[1]), 0) + starts_ref[b]
        hits = [slot == at for slot in slots]
        weight = sum(
            jnp.where(hit, gates[k : k + 1, :], 0.0) for k, hit in enumerate(hits)
        )
        gate = jnp.sum(weight, axis=1, keepdims=True)
        picked = sum(hit.astype(F32) for hit in hits).astype(BF)
        out_ref[:, :feat] = dot(picked, tokens).astype(BF)
        out_ref[:, feat:] = (gate * dot(picked, cot_ref[...])).astype(BF)


def joined(refs, columns):
    if len(refs) == 1:
        return refs[0][:, columns]
    return jnp.concatenate([ref[:, columns] for ref in refs], axis=0)


def store_rows(at_ref, first, out_ref, columns, value):
    if len(out_ref.shape) == 2:
        out_ref[:, columns] = value
        return
    count, rows = out_ref.shape[:2]
    for b in range(count):
        out_ref[at_ref[first + b], :, columns] = value[b * rows : (b + 1) * rows]


def expert_kernel(pieces, blocks, at_ref, *refs):
    ins, held = refs[:blocks], refs[blocks : blocks + 2 + pieces]
    weights = held
    if pieces == 2:
        weights = [ref for i in range(3) for ref in (held[i], held[3].at[i])]
    out_ref, d_gate_ref, d_up_ref, hidden_ref = refs[blocks + 2 + pieces :]
    feat = ins[0].shape[1] // 2
    width = feat // pieces

    def cols(p, offset):
        return pl.ds(pl.multiple_of(at_ref[p] + offset, 128), width)

    pre_gate = pre_up = grad = 0.0
    for p in range(pieces):
        part = joined(ins, cols(p, 0))
        pre_gate = pre_gate + dot(part, weights[p][...])
        pre_up = pre_up + dot(part, weights[pieces + p][...])
    sig = 1.0 / (1.0 + jnp.exp(-pre_gate))
    hidden = (pre_gate * sig * pre_up).astype(BF)
    hidden_ref[...] = hidden
    for p in range(pieces):
        down = weights[2 * pieces + p][...]
        store_rows(at_ref, pieces, out_ref, cols(p, 0), dot_last(hidden, down).astype(BF))
        grad = grad + dot(joined(ins, cols(p, feat)), down)
    d_gate = (grad * pre_up * sig * (1.0 + pre_gate * (1.0 - sig))).astype(BF)
    d_up = (grad * pre_gate * sig).astype(BF)
    d_gate_ref[...] = d_gate
    d_up_ref[...] = d_up
    for p in range(pieces):
        back = dot_last(d_gate, weights[p][...]) + dot_last(d_up, weights[pieces + p][...])
        store_rows(at_ref, pieces, out_ref, cols(p, feat), back.astype(BF))


def weights_kernel(blocks, pieces, at_ref, *refs):
    ins, outs = refs[:-pieces], refs[-pieces:]
    width = outs[0].shape[1]
    feat = ins[0].shape[1] // 2
    for p in range(pieces):
        sums = [0.0, 0.0, 0.0]
        rest = ins
        for count in blocks:
            part, rest = rest[: count + 3], rest[count + 3 :]
            rows, (d_gate, d_up, hidden) = part[:count], part[count:]
            x = joined(rows, pl.ds(pl.multiple_of(at_ref[p], 128), width))
            g = joined(rows, pl.ds(pl.multiple_of(at_ref[p] + feat, 128), width))
            sums[0] = sums[0] + dot_rows(x, d_gate[...])
            sums[1] = sums[1] + dot_rows(x, d_up[...])
            sums[2] = sums[2] + dot_rows(g, hidden[...])
        for i in range(3):
            outs[p][i] = sums[i].astype(BF)


def add_kernel(kept_ref, got_ref, *outs):
    for i, out_ref in enumerate(outs):
        out_ref[0] = kept_ref[i].astype(F32) + got_ref[i].astype(F32)


def combine_kernel(blocks, starts_ref, plan_ref, cot_ref, *refs):
    ins, (out_ref, grads_ref) = refs[:blocks], refs[blocks:]
    top = plan_ref.shape[0] // 2
    slots = plan_ref[0:top, :].astype(jnp.int32)
    gates = jnp.transpose(plan_ref[...])
    feat = cot_ref.shape[1]
    rows = joined(ins, slice(0, feat))
    cot = cot_ref[...].astype(F32)
    shape = (ins[0].shape[0], slots.shape[1])
    at = [lax.broadcasted_iota(jnp.int32, shape, 0) + starts_ref[b] for b in range(blocks)]
    at = at[0] if blocks == 1 else jnp.concatenate(at, axis=0)
    total, every = 0.0, 0.0
    lane = lax.broadcasted_iota(jnp.int32, (slots.shape[1], 128), 1)
    grads = jnp.zeros((slots.shape[1], 128), F32)
    for k in range(top):
        picked = (slots[k : k + 1, :] == at).astype(F32)
        every = every + picked
        row = dot_rows(picked.astype(BF), rows)
        total = total + gates[:, top + k : top + k + 1] * row
        grads = jnp.where(lane == k, jnp.sum(cot * row, axis=1, keepdims=True), grads)
    grads_ref[...] = jnp.transpose(grads)[0 : grads_ref.shape[0], :]
    out_ref[:, :feat] = total.astype(out_ref.dtype)
    back = dot_rows(every.astype(BF), joined(ins, slice(feat, 2 * feat)))
    out_ref[:, feat:] = back.astype(out_ref.dtype)


def finish_kernel(near_ref, far_ref, near_gg_ref, far_gg_ref, mixed_ref, grads_ref, gg_ref):
    feat = mixed_ref.shape[1]
    mixed_ref[...] = (near_ref[:, :feat] + far_ref[:, :feat].astype(F32)).astype(BF)
    grads_ref[...] = (near_ref[:, feat:] + far_ref[:, feat:].astype(F32)).astype(BF)
    gg_ref[...] = (near_gg_ref[...] + far_gg_ref[...])[0 : gg_ref.shape[0], :]


SMEM = pl.BlockSpec(memory_space=pltpu.SMEM)
VMEM = pl.BlockSpec(memory_space=pltpu.VMEM)


def near(value):
    return pltpu.with_memory_space_constraint(value, pltpu.VMEM)


def far(value):
    return pltpu.with_memory_space_constraint(value, pltpu.HBM)


def call(kernel, scalar, arrays, outs, flops):
    nbytes = sum(a.size * a.dtype.itemsize for a in arrays) if flops else 0
    return pl.pallas_call(
        kernel,
        out_shape=outs,
        in_specs=([] if scalar is None else [SMEM]) + [VMEM] * len(arrays),
        out_specs=[VMEM] * len(outs),
        compiler_params=pltpu.CompilerParams(vmem_limit_bytes=16 << 20),
        cost_estimate=cost(flops, nbytes),
    )(*([] if scalar is None else [scalar]), *arrays)


def on_device(tokens, routes, gates, gate_weight, up_weight, down_weight, cotangent):
    owners = lax.axis_size("expert")
    replicas = lax.axis_size("dp")
    tok_rows, feat = tokens.shape
    top = routes.shape[1]
    hid = gate_weight.shape[2]
    pair_count = tok_rows * top
    capacity = max(2, pair_count * 5 // (4 * owners))
    half = owners // 2
    slot_count = half * capacity
    sds = jax.ShapeDtypeStruct

    group = lax.axis_index("expert") // half
    member = lax.axis_index("expert") % half
    base = group * slot_count
    across = [(i, (i + half) % owners) for i in range(owners)]
    split = half <= 8 and half & (half - 1) == 0
    one_start = base.astype(jnp.int32).reshape(1)
    if split:
        starts = jnp.stack([base + (member ^ k) * capacity for k in range(half)])
        starts = starts.astype(jnp.int32)

    def send(rows):
        return lax.ppermute(rows, "expert", across)

    def exchange(parts):
        if len(parts) > 1:
            moved = [
                lax.ppermute(part, "expert", [(i, i ^ k) for i in range(owners)])
                for k, part in reversed(list(enumerate(parts)))
                if k
            ]
            return [parts[0], *reversed(moved)]
        moved = lax.all_to_all(
            parts[0].reshape(half, capacity, 2 * feat),
            "expert",
            split_axis=0,
            concat_axis=0,
            tiled=True,
            axis_index_groups=[list(range(half)), list(range(half, owners))],
        )
        return [moved.reshape(slot_count, 2 * feat)]

    far_cot = send(cotangent)
    own = [gate_weight[0], up_weight[0], down_weight[0]]
    share = own[0].shape[0]
    if replicas == 2:
        me = lax.axis_index("dp")
        swap = [(0, 1), (1, 0)]
        weights = [*own, lax.ppermute(jnp.stack(own), "dp", swap)]
        pieces = 2
        at = jnp.stack([me * share, (1 - me) * share]).astype(jnp.int32)
    else:
        weights = [lax.all_gather(w, "dp", axis=0, tiled=True) for w in own]
        pieces = 1
        at = jnp.zeros((1,), jnp.int32)
    width = feat // pieces

    places = jnp.concatenate([at, (starts - base) // capacity]) if split else at
    whole_rows = [pltpu.VMEM((slot_count, 2 * feat), BF)]
    split_rows = whole_rows
    if split:
        split_rows = [pltpu.HBM((capacity, 2 * feat), BF)]
        split_rows = split_rows + [pltpu.VMEM((capacity, 2 * feat), BF)] * (half - 1)
    narrow = pltpu.HBM((slot_count, hid), BF)
    first_weights = [far(w) for w in weights[:3]] + [near(w) for w in weights[3:]]
    weights = [far(w) for w in weights]
    plan_like = sds((2 * top, tok_rows), F32)
    work = 2 * slot_count * feat * hid

    def starts_of(rows):
        return starts if len(rows) > 1 else one_start

    def pick(arrays, rows, more, stretch):
        return call(
            functools.partial(pick_kernel, owners, capacity, not more),
            starts_of(rows),
            arrays,
            [*rows, plan_like, *more],
            6 * work * stretch,
        )

    def expert(rows, weights_at, stretch):
        shape = (half, *rows[0].shape) if len(rows) > 1 else rows[0].shape
        outs = call(
            functools.partial(expert_kernel, pieces, len(rows)),
            places,
            [*[near(r) for r in rows], *weights_at],
            [pltpu.VMEM(shape, BF)] + [narrow] * 3,
            6 * work * stretch,
        )
        return outs[:1], outs[1:]

    def combine(plan_at, cot_at, rows, dtype, space):
        return call(
            functools.partial(combine_kernel, len(rows)),
            starts_of(rows),
            [plan_at, cot_at, *[near(r) for r in rows]],
            [space((tok_rows, 2 * feat), dtype), pltpu.VMEM((8, tok_rows), F32)],
            6 * work * NEAR,
        )

    first = tok_rows // 2
    *near_rows, plan, parcel, rest = pick(
        [far(routes.T), far(gates.T), far(tokens), far(cotangent)],
        whole_rows,
        [pltpu.VMEM((first + 4 * top, feat), BF), pltpu.VMEM((tok_rows - first, feat), BF)],
        NEAR,
    )
    far_parcel = [near(send(parcel)), far(send(rest))]
    near_in = exchange(near_rows)
    *far_rows, far_plan = pick([*far_parcel, near(far_cot)], split_rows, [], PICK)
    far_in = exchange(far_rows)
    near_out, near_parts = expert(near_in, first_weights, EARLY)
    far_in[0], near_parts = lax.optimization_barrier((far_in[0], near_parts))
    far_out, far_parts = expert(far_in, first_weights, STRETCH)
    far_back = exchange(far_out)

    partials = call(
        functools.partial(weights_kernel, (len(near_in), len(far_in)), pieces),
        at,
        [far(x) for x in (*near_in, *near_parts, *far_in, *far_parts)],
        [pltpu.HBM((3, width, hid), BF)] * pieces,
        6 * work * NEAR,
    )
    leaving = partials[-1]
    far_back, leaving, near_out = lax.optimization_barrier((far_back, leaving, near_out))
    near_back = exchange(near_out)
    far_sum, far_gg = combine(far_plan, far(far_cot), far_back, BF, pltpu.VMEM)
    got_sum = send(far_sum)
    got_gg = send(far_gg)

    if replicas == 2:
        got = lax.ppermute(leaving, "dp", swap)
        grads = call(
            add_kernel,
            None,
            [far(partials[0]), near(got)],
            [sds((1, share, hid), F32)] * 3,
            6 * work * LATE,
        )
    else:
        got = lax.all_to_all(leaving, "dp", split_axis=1, concat_axis=0, tiled=True)
        got = got.reshape(replicas, 3, share, hid).astype(F32)
        grads = [jnp.sum(got[:, i], axis=0)[None] for i in range(3)]

    near_sum, near_gg = combine(plan, far(cotangent), near_back, F32, pltpu.VMEM)
    mixed, token_grads, gate_grads = call(
        finish_kernel,
        None,
        [near(near_sum), near(got_sum), near(near_gg), near(got_gg)],
        [sds((tok_rows, feat), BF)] * 2 + [sds((top, tok_rows), F32)],
        2 * tok_rows * feat,
    )
    return (mixed, token_grads, gate_grads.T, *grads)


def solution(mesh):
    rows = P(("dp", "expert"), None)
    weight = P("expert", "dp", None)
    return jax.shard_map(
        on_device,
        mesh=mesh,
        in_specs=(rows, rows, rows, weight, weight, weight, rows),
        out_specs=(rows, rows, rows, weight, weight, weight),
        check_vma=False,
    )
```

```python
import functools

import jax
import jax.numpy as jnp
from jax import lax
from jax.experimental import pallas as pl
from jax.experimental.pallas import tpu as pltpu
from jax.sharding import PartitionSpec as P

BF = jnp.bfloat16
F32 = jnp.float32
STRETCH = 12
NEAR = 0
PICK = 12
EARLY = 0
LATE = 12


def dot(left, right):
    return jnp.dot(left, right, preferred_element_type=F32)


def dot_rows(left, right):
    return lax.dot_general(left, right, (((0,), (0,)), ((), ())), preferred_element_type=F32)


def dot_last(left, right):
    return lax.dot_general(left, right, (((1,), (1,)), ((), ())), preferred_element_type=F32)


def cost(flops, nbytes):
    return pl.CostEstimate(flops=flops, bytes_accessed=nbytes, transcendentals=0)


def slots_in(owners, capacity, routes):
    top, rows = routes.shape
    expert = lax.broadcasted_iota(jnp.int32, (owners, rows), 0)
    named = [(routes[k : k + 1, :] == expert).astype(F32) for k in range(top)]
    onehot = sum(named)
    before = lax.broadcasted_iota(jnp.int32, (rows, rows), 0) < lax.broadcasted_iota(
        jnp.int32, (rows, rows), 1
    )
    position = dot(onehot.astype(BF), before.astype(F32).astype(BF)).astype(jnp.int32)
    return [
        routes[k : k + 1, :] * capacity
        + jnp.sum(jnp.where(routes[k : k + 1, :] == expert, position, 0), axis=0, keepdims=True)
        for k in range(top)
    ]


def pick_kernel(owners, capacity, packed, starts_ref, *refs):
    if packed:
        parcel_ref, rest_ref, cot_ref, *outs, plan_ref = refs
        top = plan_ref.shape[0] // 2
        rows, first = cot_ref.shape[0], cot_ref.shape[0] // 2
        facts = parcel_ref[first : first + 4 * top, 0:rows].astype(F32)
        routes = facts[0:top, :].astype(jnp.int32)
        gates = facts[top : 2 * top] + facts[2 * top : 3 * top] + facts[3 * top : 4 * top]
        tokens = jnp.concatenate([parcel_ref[0:first, :], rest_ref[...]], axis=0)
    else:
        routes_ref, gates_ref, tokens_ref, cot_ref, *outs, plan_ref, parcel_ref, rest_ref = refs
        top = plan_ref.shape[0] // 2
        rows, first = cot_ref.shape[0], cot_ref.shape[0] // 2
        routes, gates, tokens = routes_ref[...], gates_ref[...], tokens_ref[...]
        high = gates.astype(BF)
        after = gates - high.astype(F32)
        middle = after.astype(BF)
        low = after - middle.astype(F32)
        facts = [routes.astype(F32), high.astype(F32), middle.astype(F32), low]
        parcel_ref[0:first, :] = tokens[:first]
        rest_ref[...] = tokens[first:]
        parcel_ref[first : first + 4 * top, :] = jnp.zeros((4 * top, tokens.shape[1]), BF)
        parcel_ref[first : first + 4 * top, 0:rows] = jnp.concatenate(facts, axis=0).astype(BF)
    slots = slots_in(owners, capacity, routes)
    for k in range(top):
        plan_ref[k : k + 1, :] = slots[k].astype(F32)
    plan_ref[top : 2 * top, :] = gates
    feat = tokens.shape[1]
    for b, out_ref in enumerate(outs):
        rows = out_ref.shape[0]
        at = lax.broadcasted_iota(jnp.int32, (rows, slots[0].shape[1]), 0) + starts_ref[b]
        hits = [slot == at for slot in slots]
        weight = sum(
            jnp.where(hit, gates[k : k + 1, :], 0.0) for k, hit in enumerate(hits)
        )
        gate = jnp.sum(weight, axis=1, keepdims=True)
        picked = sum(hit.astype(F32) for hit in hits).astype(BF)
        out_ref[:, :feat] = dot(picked, tokens).astype(BF)
        out_ref[:, feat:] = (gate * dot(picked, cot_ref[...])).astype(BF)


def joined(refs, columns):
    if len(refs) == 1:
        return refs[0][:, columns]
    return jnp.concatenate([ref[:, columns] for ref in refs], axis=0)


def store_rows(at_ref, first, out_ref, columns, value):
    if len(out_ref.shape) == 2:
        out_ref[:, columns] = value
        return
    count, rows = out_ref.shape[:2]
    for b in range(count):
        out_ref[at_ref[first + b], :, columns] = value[b * rows : (b + 1) * rows]


def expert_kernel(pieces, blocks, at_ref, *refs):
    ins, held = refs[:blocks], refs[blocks : blocks + 2 + pieces]
    weights = held
    if pieces == 2:
        weights = [ref for i in range(3) for ref in (held[i], held[3].at[i])]
    out_ref, d_gate_ref, d_up_ref, hidden_ref = refs[blocks + 2 + pieces :]
    feat = ins[0].shape[1] // 2
    width = feat // pieces

    def cols(p, offset):
        return pl.ds(pl.multiple_of(at_ref[p] + offset, 128), width)

    pre_gate = pre_up = grad = 0.0
    for p in range(pieces):
        part = joined(ins, cols(p, 0))
        pre_gate = pre_gate + dot(part, weights[p][...])
        pre_up = pre_up + dot(part, weights[pieces + p][...])
    sig = 1.0 / (1.0 + jnp.exp(-pre_gate))
    hidden = (pre_gate * sig * pre_up).astype(BF)
    hidden_ref[...] = hidden
    for p in range(pieces):
        down = weights[2 * pieces + p][...]
        store_rows(at_ref, pieces, out_ref, cols(p, 0), dot_last(hidden, down).astype(BF))
        grad = grad + dot(joined(ins, cols(p, feat)), down)
    d_gate = (grad * pre_up * sig * (1.0 + pre_gate * (1.0 - sig))).astype(BF)
    d_up = (grad * pre_gate * sig).astype(BF)
    d_gate_ref[...] = d_gate
    d_up_ref[...] = d_up
    for p in range(pieces):
        back = dot_last(d_gate, weights[p][...]) + dot_last(d_up, weights[pieces + p][...])
        store_rows(at_ref, pieces, out_ref, cols(p, feat), back.astype(BF))


def weights_kernel(blocks, pieces, at_ref, *refs):
    ins, outs = refs[:-pieces], refs[-pieces:]
    width = outs[0].shape[1]
    feat = ins[0].shape[1] // 2
    for p in range(pieces):
        sums = [0.0, 0.0, 0.0]
        rest = ins
        for count in blocks:
            part, rest = rest[: count + 3], rest[count + 3 :]
            rows, (d_gate, d_up, hidden) = part[:count], part[count:]
            x = joined(rows, pl.ds(pl.multiple_of(at_ref[p], 128), width))
            g = joined(rows, pl.ds(pl.multiple_of(at_ref[p] + feat, 128), width))
            sums[0] = sums[0] + dot_rows(x, d_gate[...])
            sums[1] = sums[1] + dot_rows(x, d_up[...])
            sums[2] = sums[2] + dot_rows(g, hidden[...])
        for i in range(3):
            outs[p][i] = sums[i].astype(BF)


def add_kernel(kept_ref, got_ref, *outs):
    for i, out_ref in enumerate(outs):
        out_ref[0] = kept_ref[i].astype(F32) + got_ref[i].astype(F32)


def combine_kernel(blocks, starts_ref, plan_ref, cot_ref, *refs):
    ins, (out_ref, grads_ref) = refs[:blocks], refs[blocks:]
    top = plan_ref.shape[0] // 2
    slots = plan_ref[0:top, :].astype(jnp.int32)
    gates = jnp.transpose(plan_ref[...])
    feat = cot_ref.shape[1]
    rows = joined(ins, slice(0, feat))
    cot = cot_ref[...].astype(F32)
    shape = (ins[0].shape[0], slots.shape[1])
    at = [lax.broadcasted_iota(jnp.int32, shape, 0) + starts_ref[b] for b in range(blocks)]
    at = at[0] if blocks == 1 else jnp.concatenate(at, axis=0)
    total, every = 0.0, 0.0
    lane = lax.broadcasted_iota(jnp.int32, (slots.shape[1], 128), 1)
    grads = jnp.zeros((slots.shape[1], 128), F32)
    for k in range(top):
        picked = (slots[k : k + 1, :] == at).astype(F32)
        every = every + picked
        row = dot_rows(picked.astype(BF), rows)
        total = total + gates[:, top + k : top + k + 1] * row
        grads = jnp.where(lane == k, jnp.sum(cot * row, axis=1, keepdims=True), grads)
    grads_ref[...] = jnp.transpose(grads)[0 : grads_ref.shape[0], :]
    out_ref[:, :feat] = total.astype(out_ref.dtype)
    back = dot_rows(every.astype(BF), joined(ins, slice(feat, 2 * feat)))
    out_ref[:, feat:] = back.astype(out_ref.dtype)


def finish_kernel(near_ref, far_ref, near_gg_ref, far_gg_ref, mixed_ref, grads_ref, gg_ref):
    feat = mixed_ref.shape[1]
    mixed_ref[...] = (near_ref[:, :feat] + far_ref[:, :feat].astype(F32)).astype(BF)
    grads_ref[...] = (near_ref[:, feat:] + far_ref[:, feat:].astype(F32)).astype(BF)
    gg_ref[...] = (near_gg_ref[...] + far_gg_ref[...])[0 : gg_ref.shape[0], :]


SMEM = pl.BlockSpec(memory_space=pltpu.SMEM)
VMEM = pl.BlockSpec(memory_space=pltpu.VMEM)


def near(value):
    return pltpu.with_memory_space_constraint(value, pltpu.VMEM)


def far(value):
    return pltpu.with_memory_space_constraint(value, pltpu.HBM)


def call(kernel, scalar, arrays, outs, flops):
    nbytes = sum(a.size * a.dtype.itemsize for a in arrays) if flops else 0
    return pl.pallas_call(
        kernel,
        out_shape=outs,
        in_specs=([] if scalar is None else [SMEM]) + [VMEM] * len(arrays),
        out_specs=[VMEM] * len(outs),
        compiler_params=pltpu.CompilerParams(vmem_limit_bytes=16 << 20),
        cost_estimate=cost(flops, nbytes),
    )(*([] if scalar is None else [scalar]), *arrays)


def on_device(tokens, routes, gates, gate_weight, up_weight, down_weight, cotangent):
    owners = lax.axis_size("expert")
    replicas = lax.axis_size("dp")
    tok_rows, feat = tokens.shape
    top = routes.shape[1]
    hid = gate_weight.shape[2]
    pair_count = tok_rows * top
    capacity = max(2, pair_count * 5 // (4 * owners))
    half = owners // 2
    slot_count = half * capacity
    sds = jax.ShapeDtypeStruct

    group = lax.axis_index("expert") // half
    member = lax.axis_index("expert") % half
    base = group * slot_count
    across = [(i, (i + half) % owners) for i in range(owners)]
    split = half <= 8 and half & (half - 1) == 0
    order = [0, 4, 2, 6, 5, 3, 7, 1] if half == 8 else list(range(half))
    one_start = base.astype(jnp.int32).reshape(1)
    if split:
        starts = jnp.stack([base + (member ^ k) * capacity for k in order])
        starts = starts.astype(jnp.int32)

    def send(rows):
        return lax.ppermute(rows, "expert", across)

    def exchange(parts):
        if len(parts) > 1:
            moved = [
                lax.ppermute(part, "expert", [(i, i ^ k) for i in range(owners)])
                for k, part in zip(order, parts)
                if k
            ]
            return [parts[0], *moved]
        moved = lax.all_to_all(
            parts[0].reshape(half, capacity, 2 * feat),
            "expert",
            split_axis=0,
            concat_axis=0,
            tiled=True,
            axis_index_groups=[list(range(half)), list(range(half, owners))],
        )
        return [moved.reshape(slot_count, 2 * feat)]

    far_cot = send(cotangent)
    own = [gate_weight[0], up_weight[0], down_weight[0]]
    share = own[0].shape[0]
    if replicas == 2:
        me = lax.axis_index("dp")
        swap = [(0, 1), (1, 0)]
        weights = [*own, lax.ppermute(jnp.stack(own), "dp", swap)]
        pieces = 2
        at = jnp.stack([me * share, (1 - me) * share]).astype(jnp.int32)
    else:
        weights = [lax.all_gather(w, "dp", axis=0, tiled=True) for w in own]
        pieces = 1
        at = jnp.zeros((1,), jnp.int32)
    width = feat // pieces

    places = jnp.concatenate([at, (starts - base) // capacity]) if split else at
    whole_rows = [pltpu.VMEM((slot_count, 2 * feat), BF)]
    split_rows = whole_rows
    if split:
        split_rows = [pltpu.HBM((capacity, 2 * feat), BF)]
        split_rows = split_rows + [pltpu.VMEM((capacity, 2 * feat), BF)] * (half - 1)
    narrow = pltpu.HBM((slot_count, hid), BF)
    first_weights = [far(w) for w in weights[:3]] + [near(w) for w in weights[3:]]
    weights = [far(w) for w in weights]
    plan_like = sds((2 * top, tok_rows), F32)
    work = 2 * slot_count * feat * hid

    def starts_of(rows):
        return starts if len(rows) > 1 else one_start

    def pick(arrays, rows, more, stretch):
        return call(
            functools.partial(pick_kernel, owners, capacity, not more),
            starts_of(rows),
            arrays,
            [*rows, plan_like, *more],
            6 * work * stretch,
        )

    def expert(rows, weights_at, stretch):
        shape = (half, *rows[0].shape) if len(rows) > 1 else rows[0].shape
        outs = call(
            functools.partial(expert_kernel, pieces, len(rows)),
            places,
            [*[near(r) for r in rows], *weights_at],
            [pltpu.VMEM(shape, BF)] + [narrow] * 3,
            6 * work * stretch,
        )
        return outs[:1], outs[1:]

    def combine(plan_at, cot_at, rows, dtype, space):
        return call(
            functools.partial(combine_kernel, len(rows)),
            starts_of(rows),
            [plan_at, cot_at, *[near(r) for r in rows]],
            [space((tok_rows, 2 * feat), dtype), pltpu.VMEM((8, tok_rows), F32)],
            6 * work * NEAR,
        )

    first = tok_rows // 2
    *near_rows, plan, parcel, rest = pick(
        [far(routes.T), far(gates.T), far(tokens), far(cotangent)],
        whole_rows,
        [pltpu.VMEM((first + 4 * top, feat), BF), pltpu.VMEM((tok_rows - first, feat), BF)],
        NEAR,
    )
    far_parcel = [near(send(parcel)), far(send(rest))]
    near_in = exchange(near_rows)
    *far_rows, far_plan = pick([*far_parcel, near(far_cot)], split_rows, [], PICK)
    far_in = exchange(far_rows)
    near_out, near_parts = expert(near_in, first_weights, EARLY)
    far_in[0], near_parts = lax.optimization_barrier((far_in[0], near_parts))
    far_out, far_parts = expert(far_in, first_weights, STRETCH)
    far_back = exchange(far_out)

    partials = call(
        functools.partial(weights_kernel, (len(near_in), len(far_in)), pieces),
        at,
        [far(x) for x in (*near_in, *near_parts, *far_in, *far_parts)],
        [pltpu.HBM((3, width, hid), BF)] * pieces,
        6 * work * NEAR,
    )
    leaving = partials[-1]
    far_back, leaving, near_out = lax.optimization_barrier((far_back, leaving, near_out))
    near_back = exchange(near_out)
    far_sum, far_gg = combine(far_plan, far(far_cot), far_back, BF, pltpu.VMEM)
    got_sum = send(far_sum)
    got_gg = send(far_gg)

    if replicas == 2:
        got = lax.ppermute(leaving, "dp", swap)
        grads = call(
            add_kernel,
            None,
            [far(partials[0]), near(got)],
            [sds((1, share, hid), F32)] * 3,
            6 * work * LATE,
        )
    else:
        got = lax.all_to_all(leaving, "dp", split_axis=1, concat_axis=0, tiled=True)
        got = got.reshape(replicas, 3, share, hid).astype(F32)
        grads = [jnp.sum(got[:, i], axis=0)[None] for i in range(3)]

    near_sum, near_gg = combine(plan, far(cotangent), near_back, F32, pltpu.VMEM)
    mixed, token_grads, gate_grads = call(
        finish_kernel,
        None,
        [near(near_sum), near(got_sum), near(near_gg), near(got_gg)],
        [sds((tok_rows, feat), BF)] * 2 + [sds((top, tok_rows), F32)],
        2 * tok_rows * feat,
    )
    return (mixed, token_grads, gate_grads.T, *grads)


def solution(mesh):
    rows = P(("dp", "expert"), None)
    weight = P("expert", "dp", None)
    return jax.shard_map(
        on_device,
        mesh=mesh,
        in_specs=(rows, rows, rows, weight, weight, weight, rows),
        out_specs=(rows, rows, rows, weight, weight, weight),
        check_vma=False,
    )
```
